128 devices in a mesh: energy: 8 (over x, z_lo), momentum: 4 (over z_hi, core), atom: 4 (over y).
Axes of the slice: x: 4, y: 4, z: 4 (z_hi: 2, z_lo: 2; z = z_hi * 2 + z_lo), core: 2. Of those that a mesh axis runs over, the one named last changes fastest.
Arguments:
- green: bfloat16 [16, 32, 288, 1024], P('momentum', 'atom', None, 'energy'), may hold values from -6 to 6
- neighbours: int32 [32, 8], P('atom'), may hold values from 0 to 31, as said below
- offsets: int32 [16], replicated, may hold values from 1 to 32, as said below
- emit_weight: bfloat16 [16, 16], replicated, may hold values from 0.0099487305 to 0.099609375
- absorb_weight: bfloat16 [16, 16], replicated, may hold values from 0.0099487305 to 0.099609375
- coupling: bfloat16 [32, 8, 12, 12], P('atom'), may hold values from -1.75 to 1.75
Outputs:
- selfenergy: float32 [16, 32, 288, 1024], P('momentum', 'atom', None, 'energy')
The draws below stay inside these ranges and needn't reach their ends.
Inputs may be any that keep to these rules, and one draw needn't show every extreme that they name: `neighbours`: every entry lies within 2 of its own atom index, and some entry lies exactly 2 above it. `offsets`: all entries are distinct, and one of them equals 32.
All inputs are finite; a program needn't handle non-finite values.
Results may differ from the reference program's by a relative error of at most 0.0041.
Values may be sent and summed in bfloat16 or wider, within the bound.
A program may use at most 128 MiB of HBM per device.

```python
import math
import jax
import jax.numpy as jnp
from jax import lax

ORB = 12
NB = 8
PHON = 16
SMAX = 32
REACH = 2
KPTS = 16
ATOMS = 32
ENERGIES = 1024


def draw_neighbours(key, part):
    key_steps = jax.random.fold_in(key, 11)
    key_atom = jax.random.fold_in(key, 12)
    key_slot = jax.random.fold_in(key, 13)
    atom_ids = jnp.arange(ATOMS)[:, None]
    steps_drawn = jax.random.randint(key_steps, (ATOMS, NB), -REACH, REACH + 1)
    target = jnp.clip(atom_ids + steps_drawn, 0, ATOMS - 1)
    chosen_atom = jax.random.randint(key_atom, (), REACH, ATOMS - REACH)
    chosen_slot = jax.random.randint(key_slot, (), 0, NB)
    forced = (atom_ids == chosen_atom) & (jnp.arange(NB)[None, :] == chosen_slot)
    return jnp.where(forced, atom_ids + REACH, target).astype(jnp.int32)


def draw_offsets(key, part):
    key_order = jax.random.fold_in(key, 21)
    key_place = jax.random.fold_in(key, 22)
    ordering = jax.random.permutation(key_order, SMAX - 1) + 1
    values = jnp.concatenate([ordering[:PHON - 1], jnp.full((1,), SMAX, jnp.int32)])
    place = jax.random.randint(key_place, (), 0, PHON)
    return jnp.roll(values, place).astype(jnp.int32)


def shard_levels(rng, dims, cuts, least, high):
    level, own = 1.0, jax.random.fold_in(rng, 6)
    for position, blocks in cuts:
        heights = jnp.exp(jax.random.uniform(jax.random.fold_in(own, position), (blocks,), jnp.float32, least / len(cuts), high / len(cuts)))
        level = level * jnp.repeat(heights, dims[position] // blocks).reshape([-1 if axis == position else 1 for axis in range(len(dims))])
    return level


def bell_draw(rng, shape, scale, limit, split=(), dtype=jnp.bfloat16):
    values = jax.random.normal(rng, shape, jnp.float32) * scale
    if len(split) > 0:
        values = shard_levels(rng, shape, split, -0.22, 0.18) * values
    return jnp.clip(values, min=-limit, max=limit).astype(dtype)


def setup_inputs(seed: int = 0) -> dict:
    seeds = jax.random.split(jax.random.key(seed), 7)
    return {
        "green": bell_draw(seeds[0], (KPTS, ATOMS, 2 * ORB * ORB, ENERGIES), 1.0, 6.0, ((0, 4), (1, 4), (3, 8))),
        "neighbours": draw_neighbours(jax.random.fold_in(seeds[6], 71), 0),
        "offsets": draw_offsets(jax.random.fold_in(seeds[6], 71), 0),
        "emit_weight": jnp.clip(jnp.exp(jax.random.uniform(seeds[3], (PHON, KPTS), jnp.float32, math.log(0.0099487305), math.log(0.099609375))), 0.0099487305, 0.099609375).astype(jnp.bfloat16),
        "absorb_weight": jnp.clip(jnp.exp(jax.random.uniform(seeds[4], (PHON, KPTS), jnp.float32, math.log(0.0099487305), math.log(0.099609375))), 0.0099487305, 0.099609375).astype(jnp.bfloat16),
        "coupling": bell_draw(seeds[5], (ATOMS, NB, ORB, ORB), ORB ** -0.5, 1.75, ((0, 4),)),
    }


def reference(green, neighbours, offsets, emit_weight, absorb_weight, coupling):
    padded = jnp.pad(green.astype(jnp.float32), ((0, 0), (0, 0), (0, 0), (SMAX, SMAX)))
    lag_index = (jnp.arange(KPTS)[:, None] - jnp.arange(KPTS)[None, :]) % KPTS
    emit_full = emit_weight.astype(jnp.float32)
    absorb_full = absorb_weight.astype(jnp.float32)

    def add_mode(mode, running):
        shift = offsets[mode].astype(jnp.int32)
        early = lax.dynamic_slice_in_dim(padded, (SMAX - shift).astype(jnp.int32), ENERGIES, 3)
        later = lax.dynamic_slice_in_dim(padded, (SMAX + shift).astype(jnp.int32), ENERGIES, 3)
        emit_rows = emit_full[mode][lag_index]
        absorb_rows = absorb_full[mode][lag_index]
        running = running + jnp.einsum("pq,qaxe->paxe", emit_rows, early, precision=lax.Precision.HIGHEST)
        return running + jnp.einsum("pq,qaxe->paxe", absorb_rows, later, precision=lax.Precision.HIGHEST)

    hsum = lax.fori_loop(0, PHON, add_mode, jnp.zeros(green.shape, jnp.float32)).astype(jnp.bfloat16)
    blocks = hsum.reshape(KPTS, ATOMS, 2, ORB, ORB, ENERGIES)

    def add_slot(slot_index, accumulated):
        column = lax.dynamic_index_in_dim(neighbours, slot_index, 1, keepdims=False).astype(jnp.int32)
        chosen = jnp.take(blocks, column, axis=1).astype(jnp.float32)
        coupling_slot = lax.dynamic_index_in_dim(coupling, slot_index, 1, keepdims=False).astype(jnp.float32)
        half_block = jnp.einsum("aij,kacjle->kacile", coupling_slot, chosen).astype(jnp.bfloat16)
        return accumulated + jnp.einsum("kacile,ajl->kacije", half_block.astype(jnp.float32), coupling_slot)

    accumulated = lax.fori_loop(0, NB, add_slot, jnp.zeros(blocks.shape, jnp.float32))
    return accumulated.reshape(KPTS, ATOMS, 2 * ORB * ORB, ENERGIES)
```

```python
import functools

import jax
import jax.numpy as jnp
from jax import lax
from jax.experimental import pallas as pl
from jax.experimental.pallas import tpu as pltpu
from jax.sharding import PartitionSpec as P

ORB = 12
NB = 8
SMAX = 32
REACH = 2
KPTS = 16
PAIR = ORB * ORB
LANES = 128
SPAN = 2 * REACH + 1
MESH = pl.DeviceIdType.MESH
BF = jnp.bfloat16
F32 = jnp.float32


def place():
    e = lax.axis_index("energy")
    m = lax.axis_index("momentum")
    return e // 2, e % 2, m // 2, m % 2


def partner(t, u):
    _, zl, zh, core = place()
    far = 1 - t // 2
    flip = ((t + 1) // 2) % 2
    zh_t = zh + far * (1 - 2 * zh)
    core_t = core + flip * (1 - 2 * core)
    zl_t = zl + u * (1 - 2 * zl)
    return zh_t * 2 + core_t, zl_t


def share(chunk, m, zl):
    if chunk == 0:
        return m + 4 * (m // 2), zl
    return m + 2, zl


def exchange_kernel(
    green, offsets, emit, absorb, coupling, near,
    hout, kout,
    arrived, made, left, right, left_out, right_out,
    base, t_main, t_left, t_right, pack, kacc,
    in_send, in_recv, in_local, x_send, x_recv, out_send, out_recv, out_local, y_send, y_recv, k_sem,
):
    x, zl, zh, core = place()
    m = zh * 2 + core
    y = lax.axis_index("atom")

    def at(m_to, zl_to):
        return {"energy": x * 2 + zl_to, "momentum": m_to}

    x_left = {"energy": ((x + 3) % 4) * 2 + zl}
    x_right = {"energy": ((x + 1) % 4) * 2 + zl}
    y_left = {"atom": (y + 3) % 4}
    y_right = {"atom": (y + 1) % 4}

    barrier = pltpu.get_barrier_semaphore()
    steps = [(t, u) for t in range(4) for u in range(2) if (t, u) != (3, 0)]
    for t, u in steps:
        m_to, zl_to = partner(t, u)
        pl.semaphore_signal(barrier, inc=1, device_id=at(m_to, zl_to), device_id_type=MESH)
    for side in (x_left, x_right, y_left, y_right):
        pl.semaphore_signal(barrier, inc=1, device_id=side, device_id_type=MESH)
    pl.semaphore_wait(barrier, len(steps) + 4)

    def rows(block):
        return pl.ds(pl.multiple_of(block * PAIR, 16), PAIR)

    def send_in(chunk, t, u):
        m_to, zl_to = partner(t, u)
        atom, c = share(chunk, m_to, zl_to)
        return pltpu.make_async_remote_copy(
            src_ref=green.at[:, atom, c],
            dst_ref=arrived.at[chunk, pl.ds(m * 4, 4), rows(zl), :],
            send_sem=in_send.at[chunk, t, u],
            recv_sem=in_recv.at[chunk, t, u],
            device_id=at(m_to, zl_to),
            device_id_type=MESH,
        )

    def own_in(chunk):
        atom, c = share(chunk, m, zl)
        return pltpu.make_async_copy(
            green.at[:, atom, c], arrived.at[chunk, pl.ds(m * 4, 4), rows(zl), :], in_local.at[chunk]
        )

    for chunk in range(2):
        for t, u in steps:
            send_in(chunk, t, u).start()
        own_in(chunk).start()

    lane = lax.broadcasted_iota(jnp.int32, (KPTS, 2 * LANES), 1)
    emit_pick = (lane == offsets[...]).astype(BF)
    absorb_pick = (lane == 2 * LANES - offsets[...]).astype(BF)
    dims = (((0,), (0,)), ((), ()))
    base[...] = lax.dot_general(emit[...], emit_pick, dims, preferred_element_type=F32) + lax.dot_general(
        absorb[...], absorb_pick, dims, preferred_element_type=F32
    )
    span = LANES + 2 * SMAX

    @pl.loop(0, KPTS)
    def _(lag):
        row = jnp.broadcast_to(base[pl.ds(lag, 1), :], (span, 2 * LANES))
        block = pltpu.roll(row, 2 * LANES - SMAX, 1, stride=1, stride_axis=0)[:, :LANES].astype(BF)
        for half in range(2):
            r = (2 * KPTS + half - lag) % KPTS
            for again in range(2):
                slot = r + KPTS * again
                cols = pl.ds(half * LANES, LANES)
                t_left[pl.ds(pl.multiple_of(slot * SMAX, SMAX), SMAX), cols] = block[:SMAX]
                t_main[pl.ds(pl.multiple_of(slot * LANES, LANES), LANES), cols] = block[SMAX : SMAX + LANES]
                t_right[pl.ds(pl.multiple_of(slot * SMAX, SMAX), SMAX), cols] = block[SMAX + LANES :]

    src = lax.broadcasted_iota(jnp.int32, (4 * LANES, 2 * LANES), 0)
    dst = lax.broadcasted_iota(jnp.int32, (4 * LANES, 2 * LANES), 1)
    inner = dst % LANES
    wanted = (inner // SMAX) * LANES + inner % SMAX + (dst // LANES) * (LANES - SMAX)
    pack[...] = (src == wanted).astype(BF)

    prow = lax.broadcasted_iota(jnp.int32, (PAIR, ORB), 0)
    pcol = lax.broadcasted_iota(jnp.int32, (PAIR, ORB), 1)
    up_major = (prow // ORB == pcol).astype(BF)
    up_minor = (prow % ORB == pcol).astype(BF)
    qrow = lax.broadcasted_iota(jnp.int32, (ORB, PAIR), 0)
    qcol = lax.broadcasted_iota(jnp.int32, (ORB, PAIR), 1)
    across_major = (qcol // ORB == qrow).astype(BF)
    across_minor = (qcol % ORB == qrow).astype(BF)

    @pl.loop(0, 8)
    def _(a):
        totals = [jnp.zeros((PAIR, PAIR), F32) for _ in range(SPAN)]
        for n in range(NB):
            block = coupling[a, n]
            first = jnp.dot(block, across_major, preferred_element_type=F32).astype(BF)
            second = jnp.dot(block, across_minor, preferred_element_type=F32).astype(BF)
            first = jnp.dot(up_major, first, preferred_element_type=F32)
            second = jnp.dot(up_minor, second, preferred_element_type=F32)
            product = first * second
            step = near[a, n] - (a + y * 8) + REACH
            for d in range(SPAN):
                totals[d] = totals[d] + product * (step == d).astype(F32)
        kacc[a] = jnp.concatenate(totals, axis=1).astype(BF)

    k_copy = pltpu.make_async_copy(kacc, kout, k_sem)
    k_copy.start()

    keep_left = (x > 0).astype(F32)
    keep_right = (x < 3).astype(F32)

    def edge_copies(chunk):
        to_left = pltpu.make_async_remote_copy(
            src_ref=left_out.at[chunk], dst_ref=right.at[chunk, :, pl.ds(PAIR, PAIR), :],
            send_sem=x_send.at[chunk, 0], recv_sem=x_recv.at[chunk, 0],
            device_id=x_left, device_id_type=MESH,
        )
        to_right = pltpu.make_async_remote_copy(
            src_ref=right_out.at[chunk], dst_ref=left.at[chunk, :, pl.ds(0, PAIR), :],
            send_sem=x_send.at[chunk, 1], recv_sem=x_recv.at[chunk, 1],
            device_id=x_right, device_id_type=MESH,
        )
        return to_left, to_right

    def send_out(chunk, t, u):
        m_to, zl_to = partner(t, u)
        atom, c = share(chunk, m, zl)
        return pltpu.make_async_remote_copy(
            src_ref=made.at[chunk, pl.ds(m_to * 4, 4), rows(zl_to), :],
            dst_ref=hout.at[:, c, atom + REACH],
            send_sem=out_send.at[chunk, t, u],
            recv_sem=out_recv.at[chunk, t, u],
            device_id=at(m_to, zl_to),
            device_id_type=MESH,
        )

    def own_out(chunk):
        atom, c = share(chunk, m, zl)
        return pltpu.make_async_copy(
            made.at[chunk, pl.ds(m * 4, 4), rows(zl), :], hout.at[:, c, atom + REACH], out_local.at[chunk]
        )

    for chunk in range(2):
        for t, u in steps:
            send_in(chunk, t, u).wait_recv()
        own_in(chunk).wait()

        for group in range(4):
            four = jnp.concatenate([arrived[chunk, group * 4 + i] for i in range(4)], axis=1)
            packed = jnp.dot(four, pack[...], preferred_element_type=F32)
            left_out[chunk, group] = (packed[:PAIR, :LANES] * keep_left).astype(BF)
            left[chunk, group, PAIR:, :] = packed[:PAIR, LANES:].astype(BF)
            right[chunk, group, :PAIR, :] = packed[PAIR:, :LANES].astype(BF)
            right_out[chunk, group] = (packed[PAIR:, LANES:] * keep_right).astype(BF)
        edges = edge_copies(chunk)
        for copy in edges:
            copy.start()
        for copy in edges:
            copy.wait()

        @pl.loop(0, 4)
        def _(t):
            m_to, _ = partner(t, 0)

            @pl.loop(0, 2)
            def _(half):
                kp = m_to * 2 + half
                start = KPTS - 2 * kp
                main = jnp.concatenate([arrived[chunk, q] for q in range(KPTS)], axis=1)
                total = jnp.dot(
                    main, t_main[pl.ds(pl.multiple_of(start * LANES, LANES), KPTS * LANES), :],
                    preferred_element_type=F32,
                )
                window = pl.ds(pl.multiple_of(start * SMAX, SMAX), KPTS * SMAX)
                lows = jnp.concatenate([left[chunk, g] for g in range(4)], axis=1)
                total = total + jnp.dot(lows, t_left[window, :], preferred_element_type=F32)
                highs = jnp.concatenate([right[chunk, g] for g in range(4)], axis=1)
                total = total + jnp.dot(highs, t_right[window, :], preferred_element_type=F32)
                total = total.astype(BF)
                made[chunk, 2 * kp] = total[:, :LANES]
                made[chunk, 2 * kp + 1] = total[:, LANES:]

            send_out(chunk, t, 1).start()

            @pl.when(t < 3)
            def _():
                send_out(chunk, t, 0).start()

        own_out(chunk).start()

    def y_copies():
        down = pltpu.make_async_remote_copy(
            src_ref=hout.at[:, :, pl.ds(REACH, REACH)], dst_ref=hout.at[:, :, pl.ds(8 + REACH, REACH)],
            send_sem=y_send.at[0], recv_sem=y_recv.at[0], device_id=y_left, device_id_type=MESH,
        )
        up = pltpu.make_async_remote_copy(
            src_ref=hout.at[:, :, pl.ds(8, REACH)], dst_ref=hout.at[:, :, pl.ds(0, REACH)],
            send_sem=y_send.at[1], recv_sem=y_recv.at[1], device_id=y_right, device_id_type=MESH,
        )
        return down, up

    for t, u in steps:
        send_out(0, t, u).wait_recv()
    own_out(0).wait()
    halos = y_copies()
    for copy in halos:
        copy.start()
    for t, u in steps:
        send_out(1, t, u).wait_recv()
    own_out(1).wait()
    for copy in halos:
        copy.wait()
    k_copy.wait()
    for chunk in range(2):
        for t, u in steps:
            send_in(chunk, t, u).wait_send()
            send_out(chunk, t, u).wait_send()


def apply_kernel(h_ref, k_ref, o_ref):
    a = pl.program_id(1)
    four = [h_ref[k, 0, pl.ds(a, SPAN)].reshape(SPAN * PAIR, LANES) for k in range(4)]
    total = jnp.dot(k_ref[0], jnp.concatenate(four, axis=1), preferred_element_type=F32)
    for k in range(4):
        o_ref[k, 0, 0] = total[:, k * LANES : (k + 1) * LANES]


def shards(green, neighbours, offsets, emit_weight, absorb_weight, coupling):
    k_count, a_count, components, e_count = green.shape
    extended = a_count + 2 * REACH
    vmem = pl.BlockSpec(memory_space=pltpu.VMEM)
    hbm = pl.BlockSpec(memory_space=pl.ANY)
    dma = pltpu.SemaphoreType.DMA
    span = LANES + 2 * SMAX
    hsum, kron = pl.pallas_call(
        exchange_kernel,
        out_shape=(
            jax.ShapeDtypeStruct((k_count, 2, extended, PAIR, LANES), BF),
            jax.ShapeDtypeStruct((a_count, PAIR, SPAN * PAIR), BF),
        ),
        in_specs=[hbm, vmem, vmem, vmem, vmem, pl.BlockSpec(memory_space=pltpu.SMEM)],
        out_specs=(hbm, hbm),
        scratch_shapes=[
            pltpu.VMEM((2, KPTS, 2 * PAIR, LANES), BF),
            pltpu.VMEM((2, KPTS, 2 * PAIR, LANES), BF),
            pltpu.VMEM((2, 4, 2 * PAIR, LANES), BF),
            pltpu.VMEM((2, 4, 2 * PAIR, LANES), BF),
            pltpu.VMEM((2, 4, PAIR, LANES), BF),
            pltpu.VMEM((2, 4, PAIR, LANES), BF),
            pltpu.VMEM((KPTS, 2 * LANES), F32),
            pltpu.VMEM((2 * KPTS * LANES, 2 * LANES), BF),
            pltpu.VMEM((2 * KPTS * SMAX, 2 * LANES), BF),
            pltpu.VMEM((2 * KPTS * SMAX, 2 * LANES), BF),
            pltpu.VMEM((4 * LANES, 2 * LANES), BF),
            pltpu.VMEM((a_count, PAIR, SPAN * PAIR), BF),
            dma((2, 4, 2)), dma((2, 4, 2)), dma((2,)),
            dma((2, 2)), dma((2, 2)),
            dma((2, 4, 2)), dma((2, 4, 2)), dma((2,)),
            dma((2,)), dma((2,)), dma,
        ],
        compiler_params=pltpu.CompilerParams(
            collective_id=0, has_side_effects=True, vmem_limit_bytes=48 * 1024 * 1024
        ),
        name="exchange",
    )(
        green.reshape(k_count, a_count, 2, PAIR, e_count),
        offsets.reshape(KPTS, 1),
        emit_weight,
        absorb_weight,
        coupling,
        neighbours,
    )
    out = pl.pallas_call(
        apply_kernel,
        grid=(2, a_count),
        out_shape=jax.ShapeDtypeStruct((k_count, a_count, 2, PAIR, e_count), F32),
        in_specs=[
            pl.BlockSpec((k_count, 1, extended, PAIR, LANES), lambda c, a: (0, c, 0, 0, 0)),
            pl.BlockSpec((1, PAIR, SPAN * PAIR), lambda c, a: (a, 0, 0)),
        ],
        out_specs=pl.BlockSpec((k_count, 1, 1, PAIR, LANES), lambda c, a: (0, a, c, 0, 0)),
        compiler_params=pltpu.CompilerParams(vmem_limit_bytes=32 * 1024 * 1024),
        name="apply",
    )(hsum, kron)
    return out.reshape(k_count, a_count, components, e_count)


def solution(mesh):
    in_specs = (
        P("momentum", "atom", None, "energy"),
        P("atom", None),
        P(),
        P(),
        P(),
        P("atom", None, None, None),
    )
    out_specs = P("momentum", "atom", None, "energy")
    return jax.shard_map(shards, mesh=mesh, in_specs=in_specs, out_specs=out_specs, check_vma=False)
```

```python
import functools

import jax
import jax.numpy as jnp
from jax import lax
from jax.experimental import pallas as pl
from jax.experimental.pallas import tpu as pltpu
from jax.sharding import PartitionSpec as P

ORB = 12
NB = 8
SMAX = 32
REACH = 2
KPTS = 16
PAIR = ORB * ORB
LANES = 128
SPAN = 2 * REACH + 1
MESH = pl.DeviceIdType.MESH
BF = jnp.bfloat16
F32 = jnp.float32


def place():
    e = lax.axis_index("energy")
    m = lax.axis_index("momentum")
    return e // 2, e % 2, m // 2, m % 2


def partner(t, u):
    _, zl, zh, core = place()
    far = 1 - t // 2
    flip = ((t + 1) // 2) % 2
    zh_t = zh + far * (1 - 2 * zh)
    core_t = core + flip * (1 - 2 * core)
    zl_t = zl + u * (1 - 2 * zl)
    return zh_t * 2 + core_t, zl_t


def share(chunk, m, zl):
    if chunk == 0:
        return m + 4 * (m // 2), zl
    return m + 2, zl


def exchange_kernel(
    green, near_hbm, offsets_hbm, emit_hbm, absorb_hbm, coupling_hbm,
    out,
    arrived, made, left, right, left_out, right_out, outer, inner,
    base, t_main, t_left, t_right, pack, k_outer, k_inner,
    near, offsets, emit, absorb, coupling, ups,
    in_send, in_recv, in_local, x_send, x_recv, out_send, out_recv, out_local, y_send, y_recv, small,
):
    x, zl, zh, core = place()
    m = zh * 2 + core
    y = lax.axis_index("atom")

    def at(m_to, zl_to):
        return {"energy": x * 2 + zl_to, "momentum": m_to}

    x_left = {"energy": ((x + 3) % 4) * 2 + zl}
    x_right = {"energy": ((x + 1) % 4) * 2 + zl}
    y_left = {"atom": (y + 3) % 4}
    y_right = {"atom": (y + 1) % 4}

    barrier = pltpu.get_barrier_semaphore()
    steps = [(t, u) for t in range(4) for u in range(2) if (t, u) != (3, 0)]
    for t, u in steps:
        m_to, zl_to = partner(t, u)
        pl.semaphore_signal(barrier, inc=1, device_id=at(m_to, zl_to), device_id_type=MESH)
    for side in (x_left, x_right, y_left, y_right):
        pl.semaphore_signal(barrier, inc=1, device_id=side, device_id_type=MESH)
    fetches = [
        pltpu.make_async_copy(src, dst, small.at[i])
        for i, (src, dst) in enumerate(
            ((near_hbm, near), (offsets_hbm, offsets), (emit_hbm, emit), (absorb_hbm, absorb), (coupling_hbm, coupling))
        )
    ]
    for copy in fetches:
        copy.start()
    pl.semaphore_wait(barrier, len(steps) + 4)

    def rows(block, count=PAIR):
        return pl.ds(pl.multiple_of(block * count, 16), count)

    def send_in(chunk, t, u):
        m_to, zl_to = partner(t, u)
        atom, c = share(chunk, m_to, zl_to)
        return pltpu.make_async_remote_copy(
            src_ref=green.at[:, atom, c],
            dst_ref=arrived.at[chunk, pl.ds(m * 4, 4), rows(zl), :],
            send_sem=in_send.at[chunk, t, u],
            recv_sem=in_recv.at[chunk, t, u],
            device_id=at(m_to, zl_to),
            device_id_type=MESH,
        )

    def own_in(chunk):
        atom, c = share(chunk, m, zl)
        return pltpu.make_async_copy(
            green.at[:, atom, c], arrived.at[chunk, pl.ds(m * 4, 4), rows(zl), :], in_local.at[chunk]
        )

    for chunk in range(2):
        for t, u in steps:
            send_in(chunk, t, u).start()
        own_in(chunk).start()
    for copy in fetches:
        copy.wait()

    lane = lax.broadcasted_iota(jnp.int32, (KPTS, 2 * LANES), 1)
    line = lax.broadcasted_iota(jnp.int32, (KPTS, 2 * LANES), 0)
    shift = jnp.zeros((KPTS, 2 * LANES), jnp.int32)
    for w in range(KPTS):
        shift = jnp.where(line == w, offsets[w], shift)
    emit_pick = (lane == shift).astype(BF)
    absorb_pick = (lane == 2 * LANES - shift).astype(BF)
    dims = (((0,), (0,)), ((), ()))
    base[...] = lax.dot_general(emit[...], emit_pick, dims, preferred_element_type=F32) + lax.dot_general(
        absorb[...], absorb_pick, dims, preferred_element_type=F32
    )
    span = LANES + 2 * SMAX

    @pl.loop(0, KPTS)
    def _(lag):
        row = jnp.broadcast_to(base[pl.ds(lag, 1), :], (span, 2 * LANES))
        block = pltpu.roll(row, 2 * LANES - SMAX, 1, stride=1, stride_axis=0)[:, :LANES].astype(BF)
        for half in range(2):
            r = (2 * KPTS + half - lag) % KPTS
            for again in range(2):
                slot = r + KPTS * again
                cols = pl.ds(half * LANES, LANES)
                t_left[rows(slot, SMAX), cols] = block[:SMAX]
                t_main[rows(slot, LANES), cols] = block[SMAX : SMAX + LANES]
                t_right[rows(slot, SMAX), cols] = block[SMAX + LANES :]

    src = lax.broadcasted_iota(jnp.int32, (4 * LANES, 2 * LANES), 0)
    dst = lax.broadcasted_iota(jnp.int32, (4 * LANES, 2 * LANES), 1)
    within = dst % LANES
    wanted = (within // SMAX) * LANES + within % SMAX + (dst // LANES) * (LANES - SMAX)
    pack[...] = (src == wanted).astype(BF)

    prow = lax.broadcasted_iota(jnp.int32, (PAIR, ORB * NB), 0)
    pcol = lax.broadcasted_iota(jnp.int32, (PAIR, ORB * NB), 1)
    for n in range(NB):
        ups[n, 0] = ((prow // ORB) * NB + n == pcol).astype(BF)
        ups[n, 1] = ((prow % ORB) * NB + n == pcol).astype(BF)
    qrow = lax.broadcasted_iota(jnp.int32, (ORB, PAIR), 0)
    qcol = lax.broadcasted_iota(jnp.int32, (ORB, PAIR), 1)
    across_major = (qcol // ORB == qrow).astype(BF)
    across_minor = (qcol % ORB == qrow).astype(BF)

    @pl.loop(0, 8)
    def _(a):
        products = []
        steps_to = []
        blocks = coupling[a].reshape(ORB * NB, ORB)
        wide_major = jnp.dot(blocks, across_major, preferred_element_type=F32).astype(BF)
        wide_minor = jnp.dot(blocks, across_minor, preferred_element_type=F32).astype(BF)
        for n in range(NB):
            first = jnp.dot(ups[n, 0], wide_major, preferred_element_type=F32)
            second = jnp.dot(ups[n, 1], wide_minor, preferred_element_type=F32)
            products.append(first * second)
            steps_to.append(near[a, n] - y * 8 + REACH)
        for table, first_atom in ((k_outer, 8 * (a // 4)), (k_inner, 4)):
            parts = []
            for w in range(4):
                total = jnp.zeros((PAIR, PAIR), F32)
                for n in range(NB):
                    total = total + products[n] * (steps_to[n] == first_atom + w).astype(F32)
                parts.append(total)
            table[rows(a), :] = jnp.concatenate(parts, axis=1).astype(BF)

    keep_left = (x > 0).astype(F32)
    keep_right = (x < 3).astype(F32)

    def edge_copies(chunk):
        to_left = pltpu.make_async_remote_copy(
            src_ref=left_out.at[chunk], dst_ref=right.at[chunk, :, pl.ds(PAIR, PAIR), :],
            send_sem=x_send.at[chunk, 0], recv_sem=x_recv.at[chunk, 0],
            device_id=x_left, device_id_type=MESH,
        )
        to_right = pltpu.make_async_remote_copy(
            src_ref=right_out.at[chunk], dst_ref=left.at[chunk, :, pl.ds(0, PAIR), :],
            send_sem=x_send.at[chunk, 1], recv_sem=x_recv.at[chunk, 1],
            device_id=x_right, device_id_type=MESH,
        )
        return to_left, to_right

    def home(chunk, half):
        ks = pl.ds(2 * half, 2)
        return outer.at[ks, zl, m + REACH] if chunk == 0 else inner.at[ks, zl, m]

    def send_out(chunk, half, t, u):
        m_to, zl_to = partner(t, u)
        return pltpu.make_async_remote_copy(
            src_ref=made.at[chunk, pl.ds(m_to * 4 + 2 * half, 2), rows(zl_to), :],
            dst_ref=home(chunk, half),
            send_sem=out_send.at[chunk, half, t, u],
            recv_sem=out_recv.at[chunk, half, t, u],
            device_id=at(m_to, zl_to),
            device_id_type=MESH,
        )

    def own_out(chunk, half):
        return pltpu.make_async_copy(
            made.at[chunk, pl.ds(m * 4 + 2 * half, 2), rows(zl), :], home(chunk, half), out_local.at[chunk, half]
        )

    for chunk in range(2):
        for t, u in steps:
            send_in(chunk, t, u).wait_recv()
        own_in(chunk).wait()

        for group in range(4):
            four = jnp.concatenate([arrived[chunk, group * 4 + i] for i in range(4)], axis=1)
            packed = jnp.dot(four, pack[...], preferred_element_type=F32)
            left_out[chunk, group] = (packed[:PAIR, :LANES] * keep_left).astype(BF)
            left[chunk, group, PAIR:, :] = packed[:PAIR, LANES:].astype(BF)
            right[chunk, group, :PAIR, :] = packed[PAIR:, :LANES].astype(BF)
            right_out[chunk, group] = (packed[PAIR:, LANES:] * keep_right).astype(BF)
        edges = edge_copies(chunk)
        for copy in edges:
            copy.start()
        for copy in edges:
            copy.wait()

        @pl.loop(0, 8)
        def _(turn):
            half, t = turn // 4, turn % 4
            m_to, _ = partner(t, 0)
            kp = m_to * 2 + half
            start = KPTS - 2 * kp
            main = jnp.concatenate([arrived[chunk, q] for q in range(KPTS)], axis=1)
            total = jnp.dot(
                main, t_main[pl.ds(pl.multiple_of(start * LANES, LANES), KPTS * LANES), :],
                preferred_element_type=F32,
            )
            window = pl.ds(pl.multiple_of(start * SMAX, SMAX), KPTS * SMAX)
            lows = jnp.concatenate([left[chunk, g] for g in range(4)], axis=1)
            total = total + jnp.dot(lows, t_left[window, :], preferred_element_type=F32)
            highs = jnp.concatenate([right[chunk, g] for g in range(4)], axis=1)
            total = total + jnp.dot(highs, t_right[window, :], preferred_element_type=F32)
            total = total.astype(BF)
            made[chunk, 2 * kp] = total[:, :LANES]
            made[chunk, 2 * kp + 1] = total[:, LANES:]
            send_out(chunk, half, t, 1).start()

            @pl.when(t < 3)
            def _():
                send_out(chunk, half, t, 0).start()

            @pl.when(t == 3)
            def _():
                own_out(chunk, half).start()

    def landed(chunk, half):
        for t, u in steps:
            send_out(chunk, half, t, u).wait_recv()
        own_out(chunk, half).wait()

    def y_copies(half):
        ks = pl.ds(2 * half, 2)
        down = pltpu.make_async_remote_copy(
            src_ref=outer.at[ks, :, pl.ds(2, 2)], dst_ref=outer.at[ks, :, pl.ds(6, 2)],
            send_sem=y_send.at[half, 0], recv_sem=y_recv.at[half, 0], device_id=y_left, device_id_type=MESH,
        )
        up = pltpu.make_async_remote_copy(
            src_ref=outer.at[ks, :, pl.ds(4, 2)], dst_ref=outer.at[ks, :, pl.ds(0, 2)],
            send_sem=y_send.at[half, 1], recv_sem=y_recv.at[half, 1], device_id=y_right, device_id_type=MESH,
        )
        return down, up

    def pair_of(source, half, c, first):
        two = [source[2 * half + j, c, pl.ds(first, 4)].reshape(4 * PAIR, LANES) for j in range(2)]
        return jnp.concatenate(two, axis=1)

    def apply_outer(half):
        @pl.loop(0, 4)
        def _(turn):
            c, side = turn // 2, turn % 2
            operand = pair_of(outer, half, c, 4 * side)
            for part in range(2):
                a = 4 * side + 2 * part
                block = jnp.dot(k_outer[rows(2 * side + part, 2 * PAIR), :], operand, preferred_element_type=F32)
                for i in range(2):
                    for j in range(2):
                        out[2 * half + j, a + i, c] = block[i * PAIR : (i + 1) * PAIR, j * LANES : (j + 1) * LANES]

    def apply_inner(half):
        @pl.loop(0, 4)
        def _(turn):
            c, side = turn // 2, turn % 2
            operand = pair_of(inner, half, c, 0)
            for part in range(2):
                a = 4 * side + 2 * part
                block = jnp.dot(k_inner[rows(2 * side + part, 2 * PAIR), :], operand, preferred_element_type=F32)
                for i in range(2):
                    for j in range(2):
                        out[2 * half + j, a + i, c] += block[i * PAIR : (i + 1) * PAIR, j * LANES : (j + 1) * LANES]

    for half in range(2):
        landed(0, half)
        for copy in y_copies(half):
            copy.start()
    for half in range(2):
        for copy in y_copies(half):
            copy.wait()
        apply_outer(half)
    for chunk in range(2):
        for t, u in steps:
            send_in(chunk, t, u).wait_send()
    for half in range(2):
        landed(1, half)
        apply_inner(half)
    for chunk in range(2):
        for half in range(2):
            for t, u in steps:
                send_out(chunk, half, t, u).wait_send()


def shards(green, neighbours, offsets, emit_weight, absorb_weight, coupling):
    k_count, a_count, components, e_count = green.shape
    hbm = pl.BlockSpec(memory_space=pltpu.HBM)
    dma = pltpu.SemaphoreType.DMA
    vmem = pltpu.VMEM
    out = pl.pallas_call(
        exchange_kernel,
        out_shape=jax.ShapeDtypeStruct((k_count, a_count, 2, PAIR, e_count), F32),
        in_specs=[hbm] * 6,
        out_specs=pl.BlockSpec(memory_space=pltpu.VMEM),
        scratch_shapes=[
            vmem((2, KPTS, 2 * PAIR, LANES), BF),
            vmem((2, KPTS, 2 * PAIR, LANES), BF),
            vmem((2, 4, 2 * PAIR, LANES), BF),
            vmem((2, 4, 2 * PAIR, LANES), BF),
            vmem((2, 4, PAIR, LANES), BF),
            vmem((2, 4, PAIR, LANES), BF),
            vmem((k_count, 2, 8, PAIR, LANES), BF),
            vmem((k_count, 2, 4, PAIR, LANES), BF),
            vmem((KPTS, 2 * LANES), F32),
            vmem((2 * KPTS * LANES, 2 * LANES), BF),
            vmem((2 * KPTS * SMAX, 2 * LANES), BF),
            vmem((2 * KPTS * SMAX, 2 * LANES), BF),
            vmem((4 * LANES, 2 * LANES), BF),
            vmem((a_count * PAIR, 4 * PAIR), BF),
            vmem((a_count * PAIR, 4 * PAIR), BF),
            pltpu.SMEM((a_count, NB), jnp.int32),
            pltpu.SMEM((KPTS,), jnp.int32),
            vmem((KPTS, KPTS), BF),
            vmem((KPTS, KPTS), BF),
            vmem((a_count, ORB, NB, ORB), BF),
            vmem((NB, 2, PAIR, ORB * NB), BF),
            dma((2, 4, 2)), dma((2, 4, 2)), dma((2,)),
            dma((2, 2)), dma((2, 2)),
            dma((2, 2, 4, 2)), dma((2, 2, 4, 2)), dma((2, 2)),
            dma((2, 2)), dma((2, 2)), dma((5,)),
        ],
        compiler_params=pltpu.CompilerParams(
            collective_id=0, has_side_effects=True, vmem_limit_bytes=40 * 1024 * 1024
        ),
        name="exchange",
    )(
        *(
            pltpu.with_memory_space_constraint(array, pltpu.HBM)
            for array in (
                green.reshape(k_count, a_count, 2, PAIR, e_count),
                neighbours,
                offsets,
                emit_weight,
                absorb_weight,
                coupling.transpose(0, 2, 1, 3),
            )
        )
    )
    return out.reshape(k_count, a_count, components, e_count)


def solution(mesh):
    in_specs = (
        P("momentum", "atom", None, "energy"),
        P("atom", None),
        P(),
        P(),
        P(),
        P("atom", None, None, None),
    )
    out_specs = P("momentum", "atom", None, "energy")
    return jax.shard_map(shards, mesh=mesh, in_specs=in_specs, out_specs=out_specs, check_vma=False)
```

```python
import functools

import jax
import jax.numpy as jnp
from jax import lax
from jax.experimental import pallas as pl
from jax.experimental.pallas import tpu as pltpu
from jax.sharding import PartitionSpec as P

ORB = 12
NB = 8
SMAX = 32
REACH = 2
KPTS = 16
PAIR = ORB * ORB
LANES = 128
SPAN = 2 * REACH + 1
MESH = pl.DeviceIdType.MESH
BF = jnp.bfloat16
F32 = jnp.float32


def place():
    e = lax.axis_index("energy")
    m = lax.axis_index("momentum")
    return e // 2, e % 2, m // 2, m % 2


def partner(t, u):
    _, zl, zh, core = place()
    far = 1 - t // 2
    flip = ((t + 1) // 2) % 2
    zh_t = zh + far * (1 - 2 * zh)
    core_t = core + flip * (1 - 2 * core)
    zl_t = zl + u * (1 - 2 * zl)
    return zh_t * 2 + core_t, zl_t


def share(chunk, m, zl):
    if chunk == 0:
        return m + 4 * (m // 2), zl
    return m + 2, zl


def exchange_kernel(
    green, near_hbm, offsets_hbm, emit_hbm, absorb_hbm, coupling_hbm,
    out,
    arrived, made, left, right, left_out, right_out, outer, inner,
    base, t_main, t_left, t_right, pack, k_outer, k_inner,
    near, offsets, emit, absorb, coupling, ups,
    in_send, in_recv, in_local, x_send, x_recv, out_send, out_recv, out_local, y_send, y_recv, small,
):
    x, zl, zh, core = place()
    m = zh * 2 + core
    y = lax.axis_index("atom")

    def at(m_to, zl_to):
        return {"energy": x * 2 + zl_to, "momentum": m_to}

    x_left = {"energy": ((x + 3) % 4) * 2 + zl}
    x_right = {"energy": ((x + 1) % 4) * 2 + zl}
    y_left = {"atom": (y + 3) % 4}
    y_right = {"atom": (y + 1) % 4}

    barrier = pltpu.get_barrier_semaphore()
    steps = [(t, u) for t in range(4) for u in range(2) if (t, u) != (3, 0)]
    for t, u in steps:
        m_to, zl_to = partner(t, u)
        pl.semaphore_signal(barrier, inc=1, device_id=at(m_to, zl_to), device_id_type=MESH)
    for side in (x_left, x_right, y_left, y_right):
        pl.semaphore_signal(barrier, inc=1, device_id=side, device_id_type=MESH)
    fetches = [
        pltpu.make_async_copy(src, dst, small.at[i])
        for i, (src, dst) in enumerate(
            ((near_hbm, near), (offsets_hbm, offsets), (emit_hbm, emit), (absorb_hbm, absorb), (coupling_hbm, coupling))
        )
    ]
    for copy in fetches:
        copy.start()
    pl.semaphore_wait(barrier, len(steps) + 4)

    def rows(block, count=PAIR):
        return pl.ds(pl.multiple_of(block * count, 16), count)

    def send_in(chunk, t, u):
        m_to, zl_to = partner(t, u)
        atom, c = share(chunk, m_to, zl_to)
        return pltpu.make_async_remote_copy(
            src_ref=green.at[:, atom, c],
            dst_ref=arrived.at[chunk, pl.ds(m * 4, 4), rows(zl), :],
            send_sem=in_send.at[chunk, t, u],
            recv_sem=in_recv.at[chunk, t, u],
            device_id=at(m_to, zl_to),
            device_id_type=MESH,
        )

    def own_in(chunk):
        atom, c = share(chunk, m, zl)
        return pltpu.make_async_copy(
            green.at[:, atom, c], arrived.at[chunk, pl.ds(m * 4, 4), rows(zl), :], in_local.at[chunk]
        )

    for chunk in range(2):
        for t, u in steps:
            send_in(chunk, t, u).start()
        own_in(chunk).start()
    for copy in fetches:
        copy.wait()

    lane = lax.broadcasted_iota(jnp.int32, (KPTS, 2 * LANES), 1)
    line = lax.broadcasted_iota(jnp.int32, (KPTS, 2 * LANES), 0)
    shift = jnp.zeros((KPTS, 2 * LANES), jnp.int32)
    for w in range(KPTS):
        shift = jnp.where(line == w, offsets[w], shift)
    emit_pick = (lane == shift).astype(BF)
    absorb_pick = (lane == 2 * LANES - shift).astype(BF)
    dims = (((0,), (0,)), ((), ()))
    base[...] = lax.dot_general(emit[...], emit_pick, dims, preferred_element_type=F32) + lax.dot_general(
        absorb[...], absorb_pick, dims, preferred_element_type=F32
    )
    span = LANES + 2 * SMAX

    @pl.loop(0, KPTS)
    def _(lag):
        row = jnp.broadcast_to(base[pl.ds(lag, 1), :], (span, 2 * LANES))
        block = pltpu.roll(row, 2 * LANES - SMAX, 1, stride=1, stride_axis=0)[:, :LANES].astype(BF)
        for half in range(2):
            r = (2 * KPTS + half - lag) % KPTS
            for again in range(2):
                slot = r + KPTS * again
                cols = pl.ds(half * LANES, LANES)
                t_left[rows(slot, SMAX), cols] = block[:SMAX]
                t_main[rows(slot, LANES), cols] = block[SMAX : SMAX + LANES]
                t_right[rows(slot, SMAX), cols] = block[SMAX + LANES :]

    src = lax.broadcasted_iota(jnp.int32, (4 * LANES, 2 * LANES), 0)
    dst = lax.broadcasted_iota(jnp.int32, (4 * LANES, 2 * LANES), 1)
    within = dst % LANES
    wanted = (within // SMAX) * LANES + within % SMAX + (dst // LANES) * (LANES - SMAX)
    pack[...] = (src == wanted).astype(BF)

    prow = lax.broadcasted_iota(jnp.int32, (PAIR, ORB * NB), 0)
    pcol = lax.broadcasted_iota(jnp.int32, (PAIR, ORB * NB), 1)
    for n in range(NB):
        ups[n, 0] = ((prow // ORB) * NB + n == pcol).astype(BF)
        ups[n, 1] = ((prow % ORB) * NB + n == pcol).astype(BF)
    qrow = lax.broadcasted_iota(jnp.int32, (ORB, PAIR), 0)
    qcol = lax.broadcasted_iota(jnp.int32, (ORB, PAIR), 1)
    across_major = (qcol // ORB == qrow).astype(BF)
    across_minor = (qcol % ORB == qrow).astype(BF)

    @pl.loop(0, 8)
    def _(a):
        products = []
        steps_to = []
        blocks = coupling[a].reshape(ORB * NB, ORB)
        wide_major = jnp.dot(blocks, across_major, preferred_element_type=F32).astype(BF)
        wide_minor = jnp.dot(blocks, across_minor, preferred_element_type=F32).astype(BF)
        for n in range(NB):
            first = jnp.dot(ups[n, 0], wide_major, preferred_element_type=F32)
            second = jnp.dot(ups[n, 1], wide_minor, preferred_element_type=F32)
            products.append(first * second)
            steps_to.append(near[a, n] - y * 8 + REACH)
        for table, first_atom in ((k_outer, 8 * (a // 4)), (k_inner, 4)):
            parts = []
            for w in range(4):
                total = jnp.zeros((PAIR, PAIR), F32)
                for n in range(NB):
                    total = total + products[n] * (steps_to[n] == first_atom + w).astype(F32)
                parts.append(total)
            table[rows(a), :] = jnp.concatenate(parts, axis=1).astype(BF)

    keep_left = (x > 0).astype(F32)
    keep_right = (x < 3).astype(F32)

    def edge_copies(chunk, t):
        group, _ = partner(t, 0)
        to_left = pltpu.make_async_remote_copy(
            src_ref=left_out.at[chunk, group], dst_ref=right.at[chunk, group, pl.ds(PAIR, PAIR), :],
            send_sem=x_send.at[chunk, t, 0], recv_sem=x_recv.at[chunk, t, 0],
            device_id=x_left, device_id_type=MESH,
        )
        to_right = pltpu.make_async_remote_copy(
            src_ref=right_out.at[chunk, group], dst_ref=left.at[chunk, group, pl.ds(0, PAIR), :],
            send_sem=x_send.at[chunk, t, 1], recv_sem=x_recv.at[chunk, t, 1],
            device_id=x_right, device_id_type=MESH,
        )
        return to_left, to_right

    def home(chunk, half):
        ks = pl.ds(2 * half, 2)
        return outer.at[ks, zl, m + REACH] if chunk == 0 else inner.at[ks, zl, m]

    def send_out(chunk, half, t, u):
        m_to, zl_to = partner(t, u)
        return pltpu.make_async_remote_copy(
            src_ref=made.at[chunk, pl.ds(m_to * 4 + 2 * half, 2), rows(zl_to), :],
            dst_ref=home(chunk, half),
            send_sem=out_send.at[chunk, half, t, u],
            recv_sem=out_recv.at[chunk, half, t, u],
            device_id=at(m_to, zl_to),
            device_id_type=MESH,
        )

    def own_out(chunk, half):
        return pltpu.make_async_copy(
            made.at[chunk, pl.ds(m * 4 + 2 * half, 2), rows(zl), :], home(chunk, half), out_local.at[chunk, half]
        )

    def landed(chunk, half):
        for t, u in steps:
            send_out(chunk, half, t, u).wait_recv()
        own_out(chunk, half).wait()

    def y_copies(half):
        ks = pl.ds(2 * half, 2)
        down = pltpu.make_async_remote_copy(
            src_ref=outer.at[ks, :, pl.ds(2, 2)], dst_ref=outer.at[ks, :, pl.ds(6, 2)],
            send_sem=y_send.at[half, 0], recv_sem=y_recv.at[half, 0], device_id=y_left, device_id_type=MESH,
        )
        up = pltpu.make_async_remote_copy(
            src_ref=outer.at[ks, :, pl.ds(4, 2)], dst_ref=outer.at[ks, :, pl.ds(0, 2)],
            send_sem=y_send.at[half, 1], recv_sem=y_recv.at[half, 1], device_id=y_right, device_id_type=MESH,
        )
        return down, up

    def spread(half):
        landed(0, half)
        for copy in y_copies(half):
            copy.start()

    for chunk in range(2):
        for t in range(4):
            if t < 3:
                send_in(chunk, t, 0).wait_recv()
            else:
                own_in(chunk).wait()
            send_in(chunk, t, 1).wait_recv()
            group, _ = partner(t, 0)
            four = jnp.concatenate([arrived[chunk, group * 4 + i] for i in range(4)], axis=1)
            packed = jnp.dot(four, pack[...], preferred_element_type=F32)
            left_out[chunk, group] = (packed[:PAIR, :LANES] * keep_left).astype(BF)
            left[chunk, group, PAIR:, :] = packed[:PAIR, LANES:].astype(BF)
            right[chunk, group, :PAIR, :] = packed[PAIR:, :LANES].astype(BF)
            right_out[chunk, group] = (packed[PAIR:, LANES:] * keep_right).astype(BF)
            for copy in edge_copies(chunk, t):
                copy.start()
        for t in range(4):
            for copy in edge_copies(chunk, t):
                copy.wait()

        @pl.loop(0, 8)
        def _(turn):
            half, t = turn // 4, turn % 4
            m_to, _ = partner(t, 0)
            kp = m_to * 2 + half
            start = KPTS - 2 * kp
            main = jnp.concatenate([arrived[chunk, q] for q in range(KPTS)], axis=1)
            total = jnp.dot(
                main, t_main[pl.ds(pl.multiple_of(start * LANES, LANES), KPTS * LANES), :],
                preferred_element_type=F32,
            )
            window = pl.ds(pl.multiple_of(start * SMAX, SMAX), KPTS * SMAX)
            lows = jnp.concatenate([left[chunk, g] for g in range(4)], axis=1)
            total = total + jnp.dot(lows, t_left[window, :], preferred_element_type=F32)
            highs = jnp.concatenate([right[chunk, g] for g in range(4)], axis=1)
            total = total + jnp.dot(highs, t_right[window, :], preferred_element_type=F32)
            total = total.astype(BF)
            made[chunk, 2 * kp] = total[:, :LANES]
            made[chunk, 2 * kp + 1] = total[:, LANES:]
            send_out(chunk, half, t, 1).start()
            straight = turn < 4 if chunk == 1 else turn < 8

            @pl.when(straight & (t < 3))
            def _():
                send_out(chunk, half, t, 0).start()

            @pl.when(t == 3)
            def _():
                own_out(chunk, half).start()

            if chunk == 1:

                @pl.when(turn == 1)
                def _():
                    spread(0)

    for t in range(3):
        send_out(1, 1, t, 0).start()
    spread(1)

    def pair_of(source, half, c, first):
        two = [source[2 * half + j, c, pl.ds(first, 4)].reshape(4 * PAIR, LANES) for j in range(2)]
        return jnp.concatenate(two, axis=1)

    def apply_outer(half):
        @pl.loop(0, 4)
        def _(turn):
            c, side = turn // 2, turn % 2
            operand = pair_of(outer, half, c, 4 * side)
            for part in range(2):
                a = 4 * side + 2 * part
                block = jnp.dot(k_outer[rows(2 * side + part, 2 * PAIR), :], operand, preferred_element_type=F32)
                for i in range(2):
                    for j in range(2):
                        out[2 * half + j, a + i, c] = block[i * PAIR : (i + 1) * PAIR, j * LANES : (j + 1) * LANES]

    def apply_inner(half, c):
        @pl.loop(0, 2)
        def _(side):
            operand = pair_of(inner, half, c, 0)
            for part in range(2):
                a = 4 * side + 2 * part
                block = jnp.dot(k_inner[rows(2 * side + part, 2 * PAIR), :], operand, preferred_element_type=F32)
                for i in range(2):
                    for j in range(2):
                        out[2 * half + j, a + i, c] += block[i * PAIR : (i + 1) * PAIR, j * LANES : (j + 1) * LANES]

    for half in range(2):
        for copy in y_copies(half):
            copy.wait()
        apply_outer(half)
        for t in range(4):
            send_out(1, half, t, 1).wait_recv()
        apply_inner(half, 1 - zl)
        for t in range(3):
            send_out(1, half, t, 0).wait_recv()
        own_out(1, half).wait()
        apply_inner(half, zl)
    for chunk in range(2):
        for t, u in steps:
            send_in(chunk, t, u).wait_send()
    for chunk in range(2):
        for half in range(2):
            for t, u in steps:
                send_out(chunk, half, t, u).wait_send()


def shards(green, neighbours, offsets, emit_weight, absorb_weight, coupling):
    k_count, a_count, components, e_count = green.shape
    hbm = pl.BlockSpec(memory_space=pltpu.HBM)
    dma = pltpu.SemaphoreType.DMA
    vmem = pltpu.VMEM
    out = pl.pallas_call(
        exchange_kernel,
        out_shape=jax.ShapeDtypeStruct((k_count, a_count, 2, PAIR, e_count), F32),
        in_specs=[hbm] * 6,
        out_specs=pl.BlockSpec(memory_space=pltpu.VMEM),
        scratch_shapes=[
            vmem((2, KPTS, 2 * PAIR, LANES), BF),
            vmem((2, KPTS, 2 * PAIR, LANES), BF),
            vmem((2, 4, 2 * PAIR, LANES), BF),
            vmem((2, 4, 2 * PAIR, LANES), BF),
            vmem((2, 4, PAIR, LANES), BF),
            vmem((2, 4, PAIR, LANES), BF),
            vmem((k_count, 2, 8, PAIR, LANES), BF),
            vmem((k_count, 2, 4, PAIR, LANES), BF),
            vmem((KPTS, 2 * LANES), F32),
            vmem((2 * KPTS * LANES, 2 * LANES), BF),
            vmem((2 * KPTS * SMAX, 2 * LANES), BF),
            vmem((2 * KPTS * SMAX, 2 * LANES), BF),
            vmem((4 * LANES, 2 * LANES), BF),
            vmem((a_count * PAIR, 4 * PAIR), BF),
            vmem((a_count * PAIR, 4 * PAIR), BF),
            pltpu.SMEM((a_count, NB), jnp.int32),
            pltpu.SMEM((KPTS,), jnp.int32),
            vmem((KPTS, KPTS), BF),
            vmem((KPTS, KPTS), BF),
            vmem((a_count, ORB, NB, ORB), BF),
            vmem((NB, 2, PAIR, ORB * NB), BF),
            dma((2, 4, 2)), dma((2, 4, 2)), dma((2,)),
            dma((2, 4, 2)), dma((2, 4, 2)),
            dma((2, 2, 4, 2)), dma((2, 2, 4, 2)), dma((2, 2)),
            dma((2, 2)), dma((2, 2)), dma((5,)),
        ],
        compiler_params=pltpu.CompilerParams(
            collective_id=0, has_side_effects=True, vmem_limit_bytes=40 * 1024 * 1024
        ),
        name="exchange",
    )(
        *(
            pltpu.with_memory_space_constraint(array, pltpu.HBM)
            for array in (
                green.reshape(k_count, a_count, 2, PAIR, e_count),
                neighbours,
                offsets,
                emit_weight,
                absorb_weight,
                coupling.transpose(0, 2, 1, 3),
            )
        )
    )
    return out.reshape(k_count, a_count, components, e_count)


def solution(mesh):
    in_specs = (
        P("momentum", "atom", None, "energy"),
        P("atom", None),
        P(),
        P(),
        P(),
        P("atom", None, None, None),
    )
    out_specs = P("momentum", "atom", None, "energy")
    return jax.shard_map(shards, mesh=mesh, in_specs=in_specs, out_specs=out_specs, check_vma=False)
```

```python
import functools

import jax
import jax.numpy as jnp
from jax import lax
from jax.experimental import pallas as pl
from jax.experimental.pallas import tpu as pltpu
from jax.sharding import PartitionSpec as P

ORB = 12
NB = 8
SMAX = 32
REACH = 2
KPTS = 16
PAIR = ORB * ORB
LANES = 128
SPAN = 2 * REACH + 1
MESH = pl.DeviceIdType.MESH
BF = jnp.bfloat16
F32 = jnp.float32


def place():
    e = lax.axis_index("energy")
    m = lax.axis_index("momentum")
    return e // 2, e % 2, m // 2, m % 2


def partner(t, u):
    _, zl, zh, core = place()
    far = 1 - t // 2
    flip = ((t + 1) // 2) % 2
    zh_t = zh + far * (1 - 2 * zh)
    core_t = core + flip * (1 - 2 * core)
    zl_t = zl + u * (1 - 2 * zl)
    return zh_t * 2 + core_t, zl_t


def share(chunk, m, zl):
    if chunk == 0:
        return m + 4 * (m // 2), zl
    return m + 2, zl


def exchange_kernel(
    green, near_hbm, offsets_hbm, emit_hbm, absorb_hbm, coupling_hbm,
    out,
    arrived, made, left, right, left_out, right_out, outer, inner,
    base, t_main, t_left, t_right, pack, k_outer, k_inner,
    near, offsets, emit, absorb, coupling, ups,
    in_send, in_recv, in_local, x_send, x_recv, out_send, out_recv, out_local, y_send, y_recv, small,
    sides_in, told,
):
    x, zl, zh, core = place()
    m = zh * 2 + core
    y = lax.axis_index("atom")

    def at(m_to, zl_to):
        return {"energy": x * 2 + zl_to, "momentum": m_to}

    x_left = {"energy": ((x + 3) % 4) * 2 + zl}
    x_right = {"energy": ((x + 1) % 4) * 2 + zl}
    y_left = {"atom": (y + 3) % 4}
    y_right = {"atom": (y + 1) % 4}

    barrier = pltpu.get_barrier_semaphore()
    steps = [(t, u) for t in range(4) for u in range(2) if (t, u) != (3, 0)]
    sides = (x_left, x_right, y_left, y_right)
    head = m * 2 + zl == 0
    for t, u in steps:
        m_to, zl_to = partner(t, u)
        pl.semaphore_signal(barrier, inc=1, device_id=at(m_to, zl_to), device_id_type=MESH)

    @pl.when(head)
    def _():
        for side in sides:
            pl.semaphore_signal(barrier, inc=1, device_id=side, device_id_type=MESH)

    fetches = [
        pltpu.make_async_copy(src, dst, small.at[i])
        for i, (src, dst) in enumerate(
            ((near_hbm, near), (offsets_hbm, offsets), (emit_hbm, emit), (absorb_hbm, absorb), (coupling_hbm, coupling))
        )
    ]
    for copy in fetches:
        copy.start()
    pl.semaphore_wait(barrier, len(steps) + len(sides) * head.astype(jnp.int32))


    def rows(block, count=PAIR):
        return pl.ds(pl.multiple_of(block * count, 16), count)

    def send_in(chunk, t, u):
        m_to, zl_to = partner(t, u)
        atom, c = share(chunk, m_to, zl_to)
        return pltpu.make_async_remote_copy(
            src_ref=green.at[:, atom, c],
            dst_ref=arrived.at[chunk, pl.ds(m * 4, 4), rows(zl), :],
            send_sem=in_send.at[chunk, t, u],
            recv_sem=in_recv.at[chunk, t, u],
            device_id=at(m_to, zl_to),
            device_id_type=MESH,
        )

    def own_in(chunk):
        atom, c = share(chunk, m, zl)
        return pltpu.make_async_copy(
            green.at[:, atom, c], arrived.at[chunk, pl.ds(m * 4, 4), rows(zl), :], in_local.at[chunk]
        )

    for chunk in range(2):
        for t, u in steps:
            send_in(chunk, t, u).start()
        own_in(chunk).start()
    for copy in fetches:
        copy.wait()

    lane = lax.broadcasted_iota(jnp.int32, (KPTS, 2 * LANES), 1)
    line = lax.broadcasted_iota(jnp.int32, (KPTS, 2 * LANES), 0)
    shift = jnp.zeros((KPTS, 2 * LANES), jnp.int32)
    for w in range(KPTS):
        shift = jnp.where(line == w, offsets[w], shift)
    emit_pick = (lane == shift).astype(BF)
    absorb_pick = (lane == 2 * LANES - shift).astype(BF)
    dims = (((0,), (0,)), ((), ()))
    base[...] = lax.dot_general(emit[...], emit_pick, dims, preferred_element_type=F32) + lax.dot_general(
        absorb[...], absorb_pick, dims, preferred_element_type=F32
    )
    span = LANES + 2 * SMAX

    @pl.loop(0, KPTS)
    def _(lag):
        row = jnp.broadcast_to(base[pl.ds(lag, 1), :], (span, 2 * LANES))
        block = pltpu.roll(row, 2 * LANES - SMAX, 1, stride=1, stride_axis=0)[:, :LANES].astype(BF)
        for half in range(2):
            r = (2 * KPTS + half - lag) % KPTS
            for again in range(2):
                slot = r + KPTS * again
                cols = pl.ds(half * LANES, LANES)
                t_left[rows(slot, SMAX), cols] = block[:SMAX]
                t_main[rows(slot, LANES), cols] = block[SMAX : SMAX + LANES]
                t_right[rows(slot, SMAX), cols] = block[SMAX + LANES :]

    src = lax.broadcasted_iota(jnp.int32, (4 * LANES, 2 * LANES), 0)
    dst = lax.broadcasted_iota(jnp.int32, (4 * LANES, 2 * LANES), 1)
    within = dst % LANES
    wanted = (within // SMAX) * LANES + within % SMAX + (dst // LANES) * (LANES - SMAX)
    pack[...] = (src == wanted).astype(BF)

    prow = lax.broadcasted_iota(jnp.int32, (PAIR, ORB * NB), 0)
    pcol = lax.broadcasted_iota(jnp.int32, (PAIR, ORB * NB), 1)
    for n in range(NB):
        ups[n, 0] = ((prow // ORB) * NB + n == pcol).astype(BF)
        ups[n, 1] = ((prow % ORB) * NB + n == pcol).astype(BF)
    qrow = lax.broadcasted_iota(jnp.int32, (ORB, PAIR), 0)
    qcol = lax.broadcasted_iota(jnp.int32, (ORB, PAIR), 1)
    across_major = (qcol // ORB == qrow).astype(BF)
    across_minor = (qcol % ORB == qrow).astype(BF)

    @pl.loop(0, 8)
    def _(a):
        products = []
        steps_to = []
        blocks = coupling[a].reshape(ORB * NB, ORB)
        wide_major = jnp.dot(blocks, across_major, preferred_element_type=F32).astype(BF)
        wide_minor = jnp.dot(blocks, across_minor, preferred_element_type=F32).astype(BF)
        for n in range(NB):
            first = jnp.dot(ups[n, 0], wide_major, preferred_element_type=F32)
            second = jnp.dot(ups[n, 1], wide_minor, preferred_element_type=F32)
            products.append(first * second)
            steps_to.append(near[a, n] - y * 8 + REACH)
        for table, first_atom in ((k_outer, 8 * (a // 4)), (k_inner, 4)):
            parts = []
            for w in range(4):
                total = jnp.zeros((PAIR, PAIR), F32)
                for n in range(NB):
                    total = total + products[n] * (steps_to[n] == first_atom + w).astype(F32)
                parts.append(total)
            table[rows(a), :] = jnp.concatenate(parts, axis=1).astype(BF)

    @pl.when(head)
    def _():
        for side in sides:
            pl.semaphore_signal(sides_in, inc=1, device_id=side, device_id_type=MESH)
        pl.semaphore_wait(sides_in, len(sides))
        for t, u in steps:
            m_to, zl_to = partner(t, u)
            pl.semaphore_signal(told, inc=1, device_id=at(m_to, zl_to), device_id_type=MESH)

    @pl.when(jnp.logical_not(head))
    def _():
        pl.semaphore_wait(told, 1)

    keep_left = (x > 0).astype(F32)
    keep_right = (x < 3).astype(F32)

    def edge_copies(chunk, t):
        group, _ = partner(t, 0)
        to_left = pltpu.make_async_remote_copy(
            src_ref=left_out.at[chunk, group], dst_ref=right.at[chunk, group, pl.ds(PAIR, PAIR), :],
            send_sem=x_send.at[chunk, t, 0], recv_sem=x_recv.at[chunk, t, 0],
            device_id=x_left, device_id_type=MESH,
        )
        to_right = pltpu.make_async_remote_copy(
            src_ref=right_out.at[chunk, group], dst_ref=left.at[chunk, group, pl.ds(0, PAIR), :],
            send_sem=x_send.at[chunk, t, 1], recv_sem=x_recv.at[chunk, t, 1],
            device_id=x_right, device_id_type=MESH,
        )
        return to_left, to_right

    def home(chunk, half):
        ks = pl.ds(2 * half, 2)
        return outer.at[ks, zl, m + REACH] if chunk == 0 else inner.at[ks, zl, m]

    def send_out(chunk, half, t, u):
        m_to, zl_to = partner(t, u)
        return pltpu.make_async_remote_copy(
            src_ref=made.at[chunk, pl.ds(m_to * 4 + 2 * half, 2), rows(zl_to), :],
            dst_ref=home(chunk, half),
            send_sem=out_send.at[chunk, half, t, u],
            recv_sem=out_recv.at[chunk, half, t, u],
            device_id=at(m_to, zl_to),
            device_id_type=MESH,
        )

    def own_out(chunk, half):
        return pltpu.make_async_copy(
            made.at[chunk, pl.ds(m * 4 + 2 * half, 2), rows(zl), :], home(chunk, half), out_local.at[chunk, half]
        )

    def landed(chunk, half, part):
        if part == 0:
            for t in range(4):
                send_out(chunk, half, t, 1).wait_recv()
        else:
            for t in range(3):
                send_out(chunk, half, t, 0).wait_recv()
            own_out(chunk, half).wait()

    def c_of(part):
        return zl if part else 1 - zl

    def y_copies(half, part):
        ks, c = pl.ds(2 * half, 2), c_of(part)
        down = pltpu.make_async_remote_copy(
            src_ref=outer.at[ks, c, pl.ds(2, 2)], dst_ref=outer.at[ks, c, pl.ds(6, 2)],
            send_sem=y_send.at[half, part, 0], recv_sem=y_recv.at[half, part, 0],
            device_id=y_left, device_id_type=MESH,
        )
        up = pltpu.make_async_remote_copy(
            src_ref=outer.at[ks, c, pl.ds(4, 2)], dst_ref=outer.at[ks, c, pl.ds(0, 2)],
            send_sem=y_send.at[half, part, 1], recv_sem=y_recv.at[half, part, 1],
            device_id=y_right, device_id_type=MESH,
        )
        return down, up

    def spread(half, part):
        landed(0, half, part)
        for copy in y_copies(half, part):
            copy.start()

    for chunk in range(2):
        for t in range(4):
            if t < 3:
                send_in(chunk, t, 0).wait_recv()
            else:
                own_in(chunk).wait()
            send_in(chunk, t, 1).wait_recv()
            group, _ = partner(t, 0)
            four = jnp.concatenate([arrived[chunk, group * 4 + i] for i in range(4)], axis=1)
            packed = jnp.dot(four, pack[...], preferred_element_type=F32)
            left_out[chunk, group] = (packed[:PAIR, :LANES] * keep_left).astype(BF)
            left[chunk, group, PAIR:, :] = packed[:PAIR, LANES:].astype(BF)
            right[chunk, group, :PAIR, :] = packed[PAIR:, :LANES].astype(BF)
            right_out[chunk, group] = (packed[PAIR:, LANES:] * keep_right).astype(BF)
            for copy in edge_copies(chunk, t):
                copy.start()
        if chunk == 1:
            spread(0, 0)
        for t in range(4):
            for copy in edge_copies(chunk, t):
                copy.wait()

        @pl.loop(0, 8)
        def _(turn):
            half, t = turn // 4, turn % 4
            m_to, _ = partner(t, 0)
            kp = m_to * 2 + half
            start = KPTS - 2 * kp
            main = jnp.concatenate([arrived[chunk, q] for q in range(KPTS)], axis=1)
            total = jnp.dot(
                main, t_main[pl.ds(pl.multiple_of(start * LANES, LANES), KPTS * LANES), :],
                preferred_element_type=F32,
            )
            window = pl.ds(pl.multiple_of(start * SMAX, SMAX), KPTS * SMAX)
            lows = jnp.concatenate([left[chunk, g] for g in range(4)], axis=1)
            total = total + jnp.dot(lows, t_left[window, :], preferred_element_type=F32)
            highs = jnp.concatenate([right[chunk, g] for g in range(4)], axis=1)
            total = total + jnp.dot(highs, t_right[window, :], preferred_element_type=F32)
            total = total.astype(BF)
            made[chunk, 2 * kp] = total[:, :LANES]
            made[chunk, 2 * kp + 1] = total[:, LANES:]
            send_out(chunk, half, t, 1).start()

            @pl.when(t == 3)
            def _():
                for near_t in range(3):
                    send_out(chunk, half, near_t, 0).start()
                own_out(chunk, half).start()

            if chunk == 1:

                @pl.when(turn == 0)
                def _():
                    spread(0, 1)

                @pl.when(turn == 5)
                def _():
                    spread(1, 0)

    spread(1, 1)

    def pair_of(source, half, c, first):
        two = [source[2 * half + j, c, pl.ds(first, 4)].reshape(4 * PAIR, LANES) for j in range(2)]
        return jnp.concatenate(two, axis=1)

    def apply_outer(half, part):
        for copy in y_copies(half, part):
            copy.wait()
        c = c_of(part)

        @pl.loop(0, 2)
        def _(side):
            operand = pair_of(outer, half, c, 4 * side)
            for part in range(2):
                a = 4 * side + 2 * part
                block = jnp.dot(k_outer[rows(2 * side + part, 2 * PAIR), :], operand, preferred_element_type=F32)
                for i in range(2):
                    for j in range(2):
                        out[2 * half + j, a + i, c] = block[i * PAIR : (i + 1) * PAIR, j * LANES : (j + 1) * LANES]

    def apply_inner(half, part):
        landed(1, half, part)
        c = c_of(part)

        @pl.loop(0, 2)
        def _(side):
            operand = pair_of(inner, half, c, 0)
            for part in range(2):
                a = 4 * side + 2 * part
                block = jnp.dot(k_inner[rows(2 * side + part, 2 * PAIR), :], operand, preferred_element_type=F32)
                for i in range(2):
                    for j in range(2):
                        out[2 * half + j, a + i, c] += block[i * PAIR : (i + 1) * PAIR, j * LANES : (j + 1) * LANES]

    apply_outer(0, 0)
    apply_outer(0, 1)
    apply_inner(0, 0)
    apply_outer(1, 0)
    apply_inner(0, 1)
    apply_outer(1, 1)
    apply_inner(1, 0)
    apply_inner(1, 1)
    for chunk in range(2):
        for t, u in steps:
            send_in(chunk, t, u).wait_send()
    for chunk in range(2):
        for half in range(2):
            for t, u in steps:
                send_out(chunk, half, t, u).wait_send()


def shards(green, neighbours, offsets, emit_weight, absorb_weight, coupling):
    k_count, a_count, components, e_count = green.shape
    hbm = pl.BlockSpec(memory_space=pltpu.HBM)
    dma = pltpu.SemaphoreType.DMA
    regular = pltpu.SemaphoreType.REGULAR
    vmem = pltpu.VMEM
    out = pl.pallas_call(
        exchange_kernel,
        out_shape=jax.ShapeDtypeStruct((k_count, a_count, 2, PAIR, e_count), F32),
        in_specs=[hbm] * 6,
        out_specs=pl.BlockSpec(memory_space=pltpu.VMEM),
        scratch_shapes=[
            vmem((2, KPTS, 2 * PAIR, LANES), BF),
            vmem((2, KPTS, 2 * PAIR, LANES), BF),
            vmem((2, 4, 2 * PAIR, LANES), BF),
            vmem((2, 4, 2 * PAIR, LANES), BF),
            vmem((2, 4, PAIR, LANES), BF),
            vmem((2, 4, PAIR, LANES), BF),
            vmem((k_count, 2, 8, PAIR, LANES), BF),
            vmem((k_count, 2, 4, PAIR, LANES), BF),
            vmem((KPTS, 2 * LANES), F32),
            vmem((2 * KPTS * LANES, 2 * LANES), BF),
            vmem((2 * KPTS * SMAX, 2 * LANES), BF),
            vmem((2 * KPTS * SMAX, 2 * LANES), BF),
            vmem((4 * LANES, 2 * LANES), BF),
            vmem((a_count * PAIR, 4 * PAIR), BF),
            vmem((a_count * PAIR, 4 * PAIR), BF),
            pltpu.SMEM((a_count, NB), jnp.int32),
            pltpu.SMEM((KPTS,), jnp.int32),
            vmem((KPTS, KPTS), BF),
            vmem((KPTS, KPTS), BF),
            vmem((a_count, ORB, NB, ORB), BF),
            vmem((NB, 2, PAIR, ORB * NB), BF),
            dma((2, 4, 2)), dma((2, 4, 2)), dma((2,)),
            dma((2, 4, 2)), dma((2, 4, 2)),
            dma((2, 2, 4, 2)), dma((2, 2, 4, 2)), dma((2, 2)),
            dma((2, 2, 2)), dma((2, 2, 2)), dma((5,)),
            regular, regular,
        ],
        compiler_params=pltpu.CompilerParams(
            collective_id=0, has_side_effects=True, vmem_limit_bytes=40 * 1024 * 1024
        ),
        name="exchange",
    )(
        *(
            pltpu.with_memory_space_constraint(array, pltpu.HBM)
            for array in (
                green.reshape(k_count, a_count, 2, PAIR, e_count),
                neighbours,
                offsets,
                emit_weight,
                absorb_weight,
                coupling.transpose(0, 2, 1, 3),
            )
        )
    )
    return out.reshape(k_count, a_count, components, e_count)


def solution(mesh):
    in_specs = (
        P("momentum", "atom", None, "energy"),
        P("atom", None),
        P(),
        P(),
        P(),
        P("atom", None, None, None),
    )
    out_specs = P("momentum", "atom", None, "energy")
    return jax.shard_map(shards, mesh=mesh, in_specs=in_specs, out_specs=out_specs, check_vma=False)
```

```python
import functools

import jax
import jax.numpy as jnp
from jax import lax
from jax.experimental import pallas as pl
from jax.experimental.pallas import tpu as pltpu
from jax.sharding import PartitionSpec as P

ORB = 12
NB = 8
SMAX = 32
REACH = 2
KPTS = 16
PAIR = ORB * ORB
LANES = 128
SPAN = 2 * REACH + 1
MESH = pl.DeviceIdType.MESH
BF = jnp.bfloat16
F32 = jnp.float32


def place():
    e = lax.axis_index("energy")
    m = lax.axis_index("momentum")
    return e // 2, e % 2, m // 2, m % 2


def partner(t, u):
    _, zl, zh, core = place()
    far = 1 - t // 2
    flip = ((t + 1) // 2) % 2
    zh_t = zh + far * (1 - 2 * zh)
    core_t = core + flip * (1 - 2 * core)
    zl_t = zl + u * (1 - 2 * zl)
    return zh_t * 2 + core_t, zl_t


def share(chunk, m, zl):
    if chunk == 0:
        return m + 4 * (m // 2), zl
    return m + 2, zl


def exchange_kernel(
    green_hbm, near_hbm, offsets_hbm, emit_hbm, absorb_hbm, coupling_hbm,
    out, inner, k_inner,
    arrived, made, left, right, left_out, right_out, outer,
    base, t_main, t_left, t_right, pack, k_outer,
    near, offsets, emit, absorb, coupling, ups, green,
    in_send, in_recv, in_local, x_send, x_recv, out_send, out_recv, out_local, y_send, y_recv, small,
    sides_in, told,
):
    x, zl, zh, core = place()
    m = zh * 2 + core
    y = lax.axis_index("atom")

    def at(m_to, zl_to):
        return {"energy": x * 2 + zl_to, "momentum": m_to}

    x_left = {"energy": ((x + 3) % 4) * 2 + zl}
    x_right = {"energy": ((x + 1) % 4) * 2 + zl}
    y_left = {"atom": (y + 3) % 4}
    y_right = {"atom": (y + 1) % 4}

    barrier = pltpu.get_barrier_semaphore()
    steps = [(t, u) for t in range(4) for u in range(2) if (t, u) != (3, 0)]
    prefetch = pltpu.make_async_copy(green_hbm, green, small.at[5])
    prefetch.start()
    sides = (x_left, x_right, y_left, y_right)
    head = m * 2 + zl == 0
    for t, u in steps:
        m_to, zl_to = partner(t, u)
        pl.semaphore_signal(barrier, inc=1, device_id=at(m_to, zl_to), device_id_type=MESH)

    @pl.when(head)
    def _():
        for side in sides:
            pl.semaphore_signal(barrier, inc=1, device_id=side, device_id_type=MESH)

    fetches = [
        pltpu.make_async_copy(src, dst, small.at[i])
        for i, (src, dst) in enumerate(
            ((near_hbm, near), (offsets_hbm, offsets), (emit_hbm, emit), (absorb_hbm, absorb), (coupling_hbm, coupling))
        )
    ]
    for copy in fetches:
        copy.start()
    prefetch.wait()
    pl.semaphore_wait(barrier, len(steps) + len(sides) * head.astype(jnp.int32))


    def rows(block, count=PAIR):
        return pl.ds(pl.multiple_of(block * count, 16), count)

    def send_in(chunk, t, u):
        m_to, zl_to = partner(t, u)
        atom, c = share(chunk, m_to, zl_to)
        return pltpu.make_async_remote_copy(
            src_ref=green.at[:, atom, c],
            dst_ref=arrived.at[chunk, pl.ds(m * 4, 4), rows(zl), :],
            send_sem=in_send.at[chunk, t, u],
            recv_sem=in_recv.at[chunk, t, u],
            device_id=at(m_to, zl_to),
            device_id_type=MESH,
        )

    def own_in(chunk):
        atom, c = share(chunk, m, zl)
        return pltpu.make_async_copy(
            green.at[:, atom, c], arrived.at[chunk, pl.ds(m * 4, 4), rows(zl), :], in_local.at[chunk]
        )

    for chunk in range(2):
        for t, u in steps:
            send_in(chunk, t, u).start()
        own_in(chunk).start()
    for copy in fetches:
        copy.wait()

    lane = lax.broadcasted_iota(jnp.int32, (KPTS, 2 * LANES), 1)
    line = lax.broadcasted_iota(jnp.int32, (KPTS, 2 * LANES), 0)
    shift = jnp.zeros((KPTS, 2 * LANES), jnp.int32)
    for w in range(KPTS):
        shift = jnp.where(line == w, offsets[w], shift)
    emit_pick = (lane == shift).astype(BF)
    absorb_pick = (lane == 2 * LANES - shift).astype(BF)
    dims = (((0,), (0,)), ((), ()))
    base[...] = lax.dot_general(emit[...], emit_pick, dims, preferred_element_type=F32) + lax.dot_general(
        absorb[...], absorb_pick, dims, preferred_element_type=F32
    )
    span = LANES + 2 * SMAX

    @pl.loop(0, KPTS)
    def _(lag):
        row = jnp.broadcast_to(base[pl.ds(lag, 1), :], (span, 2 * LANES))
        block = pltpu.roll(row, 2 * LANES - SMAX, 1, stride=1, stride_axis=0)[:, :LANES].astype(BF)
        for half in range(2):
            r = (2 * KPTS + half - lag) % KPTS
            for again in range(2):
                slot = r + KPTS * again
                cols = pl.ds(half * LANES, LANES)
                t_left[rows(slot, SMAX), cols] = block[:SMAX]
                t_main[rows(slot, LANES), cols] = block[SMAX : SMAX + LANES]
                t_right[rows(slot, SMAX), cols] = block[SMAX + LANES :]

    src = lax.broadcasted_iota(jnp.int32, (4 * LANES, 2 * LANES), 0)
    dst = lax.broadcasted_iota(jnp.int32, (4 * LANES, 2 * LANES), 1)
    within = dst % LANES
    wanted = (within // SMAX) * LANES + within % SMAX + (dst // LANES) * (LANES - SMAX)
    pack[...] = (src == wanted).astype(BF)

    prow = lax.broadcasted_iota(jnp.int32, (PAIR, ORB * NB), 0)
    pcol = lax.broadcasted_iota(jnp.int32, (PAIR, ORB * NB), 1)
    for n in range(NB):
        ups[n, 0] = ((prow // ORB) * NB + n == pcol).astype(BF)
        ups[n, 1] = ((prow % ORB) * NB + n == pcol).astype(BF)
    qrow = lax.broadcasted_iota(jnp.int32, (ORB, PAIR), 0)
    qcol = lax.broadcasted_iota(jnp.int32, (ORB, PAIR), 1)
    across_major = (qcol // ORB == qrow).astype(BF)
    across_minor = (qcol % ORB == qrow).astype(BF)

    @pl.loop(0, 8)
    def _(a):
        products = []
        steps_to = []
        blocks = coupling[a].reshape(ORB * NB, ORB)
        wide_major = jnp.dot(blocks, across_major, preferred_element_type=F32).astype(BF)
        wide_minor = jnp.dot(blocks, across_minor, preferred_element_type=F32).astype(BF)
        for n in range(NB):
            first = jnp.dot(ups[n, 0], wide_major, preferred_element_type=F32)
            second = jnp.dot(ups[n, 1], wide_minor, preferred_element_type=F32)
            products.append(first * second)
            steps_to.append(near[a, n] - y * 8 + REACH)
        for table, first_atom in ((k_outer, 8 * (a // 4)), (k_inner, 4)):
            parts = []
            for w in range(4):
                total = jnp.zeros((PAIR, PAIR), F32)
                for n in range(NB):
                    total = total + products[n] * (steps_to[n] == first_atom + w).astype(F32)
                parts.append(total)
            table[rows(a), :] = jnp.concatenate(parts, axis=1).astype(BF)

    @pl.when(head)
    def _():
        for side in sides:
            pl.semaphore_signal(sides_in, inc=1, device_id=side, device_id_type=MESH)
        pl.semaphore_wait(sides_in, len(sides))
        for t, u in steps:
            m_to, zl_to = partner(t, u)
            pl.semaphore_signal(told, inc=1, device_id=at(m_to, zl_to), device_id_type=MESH)

    @pl.when(jnp.logical_not(head))
    def _():
        pl.semaphore_wait(told, 1)

    keep_left = (x > 0).astype(F32)
    keep_right = (x < 3).astype(F32)

    def edge_copies(chunk, t):
        group, _ = partner(t, 0)
        to_left = pltpu.make_async_remote_copy(
            src_ref=left_out.at[chunk, group], dst_ref=right.at[chunk, group, pl.ds(PAIR, PAIR), :],
            send_sem=x_send.at[chunk, t, 0], recv_sem=x_recv.at[chunk, t, 0],
            device_id=x_left, device_id_type=MESH,
        )
        to_right = pltpu.make_async_remote_copy(
            src_ref=right_out.at[chunk, group], dst_ref=left.at[chunk, group, pl.ds(0, PAIR), :],
            send_sem=x_send.at[chunk, t, 1], recv_sem=x_recv.at[chunk, t, 1],
            device_id=x_right, device_id_type=MESH,
        )
        return to_left, to_right

    def home(chunk, half):
        ks = pl.ds(2 * half, 2)
        return outer.at[ks, zl, m + REACH] if chunk == 0 else inner.at[ks, zl, m]

    def send_out(chunk, half, t, u):
        m_to, zl_to = partner(t, u)
        return pltpu.make_async_remote_copy(
            src_ref=made.at[chunk, pl.ds(m_to * 4 + 2 * half, 2), rows(zl_to), :],
            dst_ref=home(chunk, half),
            send_sem=out_send.at[chunk, half, t, u],
            recv_sem=out_recv.at[chunk, half, t, u],
            device_id=at(m_to, zl_to),
            device_id_type=MESH,
        )

    def own_out(chunk, half):
        return pltpu.make_async_copy(
            made.at[chunk, pl.ds(m * 4 + 2 * half, 2), rows(zl), :], home(chunk, half), out_local.at[chunk, half]
        )

    def landed(chunk, half, part):
        if part == 1:
            for t in range(4):
                send_out(chunk, half, t, 1).wait_recv()
        else:
            for t in range(3):
                send_out(chunk, half, t, 0).wait_recv()
            own_out(chunk, half).wait()

    def c_of(part):
        return 1 - zl if part else zl

    def y_copies(half, part):
        ks, c = pl.ds(2 * half, 2), c_of(part)
        down = pltpu.make_async_remote_copy(
            src_ref=outer.at[ks, c, pl.ds(2, 2)], dst_ref=outer.at[ks, c, pl.ds(6, 2)],
            send_sem=y_send.at[half, part, 0], recv_sem=y_recv.at[half, part, 0],
            device_id=y_left, device_id_type=MESH,
        )
        up = pltpu.make_async_remote_copy(
            src_ref=outer.at[ks, c, pl.ds(4, 2)], dst_ref=outer.at[ks, c, pl.ds(0, 2)],
            send_sem=y_send.at[half, part, 1], recv_sem=y_recv.at[half, part, 1],
            device_id=y_right, device_id_type=MESH,
        )
        return down, up

    def spread(half, part):
        landed(0, half, part)
        for copy in y_copies(half, part):
            copy.start()

    for chunk in range(2):
        for t in range(4):
            if t < 3:
                send_in(chunk, t, 0).wait_recv()
            else:
                own_in(chunk).wait()
            send_in(chunk, t, 1).wait_recv()
            group, _ = partner(t, 0)
            four = jnp.concatenate([arrived[chunk, group * 4 + i] for i in range(4)], axis=1)
            packed = jnp.dot(four, pack[...], preferred_element_type=F32)
            left_out[chunk, group] = (packed[:PAIR, :LANES] * keep_left).astype(BF)
            left[chunk, group, PAIR:, :] = packed[:PAIR, LANES:].astype(BF)
            right[chunk, group, :PAIR, :] = packed[PAIR:, :LANES].astype(BF)
            right_out[chunk, group] = (packed[PAIR:, LANES:] * keep_right).astype(BF)
            for copy in edge_copies(chunk, t):
                copy.start()
        if chunk == 1:
            spread(0, 0)
        for t in range(4):
            for copy in edge_copies(chunk, t):
                copy.wait()

        @pl.loop(0, 8)
        def _(turn):
            half, t = turn // 4, turn % 4
            m_to, _ = partner(t, 0)
            kp = m_to * 2 + half
            start = KPTS - 2 * kp
            main = jnp.concatenate([arrived[chunk, q] for q in range(KPTS)], axis=1)
            total = jnp.dot(
                main, t_main[pl.ds(pl.multiple_of(start * LANES, LANES), KPTS * LANES), :],
                preferred_element_type=F32,
            )
            window = pl.ds(pl.multiple_of(start * SMAX, SMAX), KPTS * SMAX)
            lows = jnp.concatenate([left[chunk, g] for g in range(4)], axis=1)
            total = total + jnp.dot(lows, t_left[window, :], preferred_element_type=F32)
            highs = jnp.concatenate([right[chunk, g] for g in range(4)], axis=1)
            total = total + jnp.dot(highs, t_right[window, :], preferred_element_type=F32)
            total = total.astype(BF)
            made[chunk, 2 * kp] = total[:, :LANES]
            made[chunk, 2 * kp + 1] = total[:, LANES:]

            @pl.when(t < 3)
            def _():
                send_out(chunk, half, t, 0).start()

            @pl.when(t == 3)
            def _():
                own_out(chunk, half).start()
                for near_t in range(4):
                    send_out(chunk, half, near_t, 1).start()

            if chunk == 1:

                @pl.when(turn == 0)
                def _():
                    spread(0, 1)

                @pl.when(turn == 5)
                def _():
                    spread(1, 0)

    spread(1, 1)

    def pair_of(source, half, c, first):
        two = [source[2 * half + j, c, pl.ds(first, 4)].reshape(4 * PAIR, LANES) for j in range(2)]
        return jnp.concatenate(two, axis=1)

    def apply_outer(half, part):
        for copy in y_copies(half, part):
            copy.wait()
        c = c_of(part)

        @pl.loop(0, 2)
        def _(side):
            operand = pair_of(outer, half, c, 4 * side)
            for part in range(2):
                a = 4 * side + 2 * part
                block = jnp.dot(k_outer[rows(2 * side + part, 2 * PAIR), :], operand, preferred_element_type=F32)
                for i in range(2):
                    for j in range(2):
                        out[2 * half + j, a + i, c] = block[i * PAIR : (i + 1) * PAIR, j * LANES : (j + 1) * LANES]

    def apply_inner(half, part):
        landed(1, half, part)
        c = c_of(part)

        @pl.loop(0, 2)
        def _(side):
            operand = pair_of(inner, half, c, 0)
            for part in range(2):
                a = 4 * side + 2 * part
                block = jnp.dot(k_inner[rows(2 * side + part, 2 * PAIR), :], operand, preferred_element_type=F32)
                for i in range(2):
                    for j in range(2):
                        out[2 * half + j, a + i, c] += block[i * PAIR : (i + 1) * PAIR, j * LANES : (j + 1) * LANES]

    apply_outer(0, 0)
    apply_outer(0, 1)
    apply_inner(0, 0)
    apply_outer(1, 0)
    apply_inner(0, 1)
    apply_outer(1, 1)
    apply_inner(1, 0)
    landed(1, 1, 1)
    for chunk in range(2):
        for t, u in steps:
            send_in(chunk, t, u).wait_send()
    for chunk in range(2):
        for half in range(2):
            for t, u in steps:
                send_out(chunk, half, t, u).wait_send()


def finish_kernel(most, last, k_inner, out, block, sems):
    c = 1 - lax.axis_index("energy") % 2
    first = pl.ds(0, 2)
    second = pl.ds(2, 2)
    copies = [
        pltpu.make_async_copy(most.at[first], out.at[first], sems.at[0]),
        pltpu.make_async_copy(most.at[second, :, 1 - c], out.at[second, :, 1 - c], sems.at[1]),
    ]
    for copy in copies:
        copy.start()
    operand = jnp.concatenate([last[2 + j, c].reshape(4 * PAIR, LANES) for j in range(2)], axis=1)
    for side in range(2):
        for part in range(2):
            a = 4 * side + 2 * part
            product = jnp.dot(k_inner[a * PAIR : (a + 2) * PAIR, :], operand, preferred_element_type=F32)
            for i in range(2):
                for j in range(2):
                    block[j, a + i] = most[2 + j, a + i, c] + product[i * PAIR : (i + 1) * PAIR, j * LANES : (j + 1) * LANES]
        atoms = pl.ds(4 * side, 4)
        copy = pltpu.make_async_copy(block.at[:, atoms], out.at[second, atoms, c], sems.at[2 + side])
        copy.start()
        copies.append(copy)
    for copy in copies:
        copy.wait()


def shards(green, neighbours, offsets, emit_weight, absorb_weight, coupling):
    k_count, a_count, components, e_count = green.shape
    hbm = pl.BlockSpec(memory_space=pltpu.HBM)
    dma = pltpu.SemaphoreType.DMA
    regular = pltpu.SemaphoreType.REGULAR
    vmem = pltpu.VMEM
    shape = jax.ShapeDtypeStruct((k_count, a_count, 2, PAIR, e_count), F32)
    in_vmem = pl.BlockSpec(memory_space=vmem)
    most, last, k_inner = pl.pallas_call(
        exchange_kernel,
        out_shape=(
            shape,
            jax.ShapeDtypeStruct((k_count, 2, 4, PAIR, LANES), BF),
            jax.ShapeDtypeStruct((a_count * PAIR, 4 * PAIR), BF),
        ),
        in_specs=[hbm] * 6,
        out_specs=(in_vmem,) * 3,
        scratch_shapes=[
            vmem((2, KPTS, 2 * PAIR, LANES), BF),
            vmem((2, KPTS, 2 * PAIR, LANES), BF),
            vmem((2, 4, 2 * PAIR, LANES), BF),
            vmem((2, 4, 2 * PAIR, LANES), BF),
            vmem((2, 4, PAIR, LANES), BF),
            vmem((2, 4, PAIR, LANES), BF),
            vmem((k_count, 2, 8, PAIR, LANES), BF),
            vmem((KPTS, 2 * LANES), F32),
            vmem((2 * KPTS * LANES, 2 * LANES), BF),
            vmem((2 * KPTS * SMAX, 2 * LANES), BF),
            vmem((2 * KPTS * SMAX, 2 * LANES), BF),
            vmem((4 * LANES, 2 * LANES), BF),
            vmem((a_count * PAIR, 4 * PAIR), BF),
            pltpu.SMEM((a_count, NB), jnp.int32),
            pltpu.SMEM((KPTS,), jnp.int32),
            vmem((KPTS, KPTS), BF),
            vmem((KPTS, KPTS), BF),
            vmem((a_count, ORB, NB, ORB), BF),
            vmem((NB, 2, PAIR, ORB * NB), BF),
            vmem((k_count, a_count, 2, PAIR, LANES), BF),
            dma((2, 4, 2)), dma((2, 4, 2)), dma((2,)),
            dma((2, 4, 2)), dma((2, 4, 2)),
            dma((2, 2, 4, 2)), dma((2, 2, 4, 2)), dma((2, 2)),
            dma((2, 2, 2)), dma((2, 2, 2)), dma((6,)),
            regular, regular,
        ],
        compiler_params=pltpu.CompilerParams(
            collective_id=0, has_side_effects=True, vmem_limit_bytes=40 * 1024 * 1024
        ),
        name="exchange",
    )(
        *(
            pltpu.with_memory_space_constraint(array, pltpu.HBM)
            for array in (
                green.reshape(k_count, a_count, 2, PAIR, e_count),
                neighbours,
                offsets,
                emit_weight,
                absorb_weight,
                coupling.transpose(0, 2, 1, 3),
            )
        )
    )
    out = pl.pallas_call(
        finish_kernel,
        out_shape=shape,
        in_specs=[in_vmem] * 3,
        out_specs=hbm,
        scratch_shapes=[vmem((2, a_count, PAIR, LANES), F32), dma((4,))],
        compiler_params=pltpu.CompilerParams(vmem_limit_bytes=8 * 1024 * 1024),
        name="finish",
    )(most, last, k_inner)
    return out.reshape(k_count, a_count, components, e_count)


def solution(mesh):
    in_specs = (
        P("momentum", "atom", None, "energy"),
        P("atom", None),
        P(),
        P(),
        P(),
        P("atom", None, None, None),
    )
    out_specs = P("momentum", "atom", None, "energy")
    return jax.shard_map(shards, mesh=mesh, in_specs=in_specs, out_specs=out_specs, check_vma=False)
```

```python
import functools

import jax
import jax.numpy as jnp
from jax import lax
from jax.experimental import pallas as pl
from jax.experimental.pallas import tpu as pltpu
from jax.sharding import PartitionSpec as P

ORB = 12
NB = 8
SMAX = 32
REACH = 2
KPTS = 16
PAIR = ORB * ORB
LANES = 128
SPAN = 2 * REACH + 1
MESH = pl.DeviceIdType.MESH
BF = jnp.bfloat16
F32 = jnp.float32


def place():
    e = lax.axis_index("energy")
    m = lax.axis_index("momentum")
    return e // 2, e % 2, m // 2, m % 2


def partner(t, u):
    _, zl, zh, core = place()
    far = 1 - t // 2
    flip = ((t + 1) // 2) % 2
    zh_t = zh + far * (1 - 2 * zh)
    core_t = core + flip * (1 - 2 * core)
    zl_t = zl + u * (1 - 2 * zl)
    return zh_t * 2 + core_t, zl_t


def share(chunk, m, zl):
    if chunk == 0:
        return m + 4 * (m // 2), zl
    return m + 2, zl


def exchange_kernel(
    green_hbm, near_hbm, offsets_hbm, emit_hbm, absorb_hbm, coupling_hbm,
    out, inner, k_inner,
    arrived, made, left, right, left_out, right_out, outer,
    base, t_main, t_left, t_right, pack, k_outer,
    near, offsets, emit, absorb, coupling, ups, green,
    in_send, in_recv, in_local, x_send, x_recv, out_send, out_recv, out_local, y_send, y_recv, small,
    sides_in, told,
):
    x, zl, zh, core = place()
    m = zh * 2 + core
    y = lax.axis_index("atom")

    def at(m_to, zl_to):
        return {"energy": x * 2 + zl_to, "momentum": m_to}

    x_left = {"energy": ((x + 3) % 4) * 2 + zl}
    x_right = {"energy": ((x + 1) % 4) * 2 + zl}
    y_left = {"atom": (y + 3) % 4}
    y_right = {"atom": (y + 1) % 4}

    barrier = pltpu.get_barrier_semaphore()
    steps = [(t, u) for t in range(4) for u in range(2) if (t, u) != (3, 0)]
    prefetch = pltpu.make_async_copy(green_hbm, green, small.at[5])
    prefetch.start()
    sides = (x_left, x_right, y_left, y_right)
    head = m * 2 + zl == 0
    for t, u in steps:
        m_to, zl_to = partner(t, u)
        pl.semaphore_signal(barrier, inc=1, device_id=at(m_to, zl_to), device_id_type=MESH)

    @pl.when(head)
    def _():
        for side in sides:
            pl.semaphore_signal(barrier, inc=1, device_id=side, device_id_type=MESH)

    fetches = [
        pltpu.make_async_copy(src, dst, small.at[i])
        for i, (src, dst) in enumerate(
            ((near_hbm, near), (offsets_hbm, offsets), (emit_hbm, emit), (absorb_hbm, absorb), (coupling_hbm, coupling))
        )
    ]
    for copy in fetches:
        copy.start()
    prefetch.wait()
    pl.semaphore_wait(barrier, len(steps) + len(sides) * head.astype(jnp.int32))


    def rows(block, count=PAIR):
        return pl.ds(pl.multiple_of(block * count, 16), count)

    def send_in(chunk, t, u):
        m_to, zl_to = partner(t, u)
        atom, c = share(chunk, m_to, zl_to)
        return pltpu.make_async_remote_copy(
            src_ref=green.at[:, atom, c],
            dst_ref=arrived.at[chunk, pl.ds(m * 4, 4), rows(zl), :],
            send_sem=in_send.at[chunk, t, u],
            recv_sem=in_recv.at[chunk, t, u],
            device_id=at(m_to, zl_to),
            device_id_type=MESH,
        )

    def own_in(chunk):
        atom, c = share(chunk, m, zl)
        return pltpu.make_async_copy(
            green.at[:, atom, c], arrived.at[chunk, pl.ds(m * 4, 4), rows(zl), :], in_local.at[chunk]
        )

    for chunk in range(2):
        for t, u in steps:
            send_in(chunk, t, u).start()
        own_in(chunk).start()
    for copy in fetches:
        copy.wait()

    lane = lax.broadcasted_iota(jnp.int32, (KPTS, 2 * LANES), 1)
    line = lax.broadcasted_iota(jnp.int32, (KPTS, 2 * LANES), 0)
    shift = jnp.zeros((KPTS, 2 * LANES), jnp.int32)
    for w in range(KPTS):
        shift = jnp.where(line == w, offsets[w], shift)
    emit_pick = (lane == shift).astype(BF)
    absorb_pick = (lane == 2 * LANES - shift).astype(BF)
    dims = (((0,), (0,)), ((), ()))
    base[...] = lax.dot_general(emit[...], emit_pick, dims, preferred_element_type=F32) + lax.dot_general(
        absorb[...], absorb_pick, dims, preferred_element_type=F32
    )
    span = LANES + 2 * SMAX

    @pl.loop(0, KPTS)
    def _(lag):
        row = jnp.broadcast_to(base[pl.ds(lag, 1), :], (span, 2 * LANES))
        block = pltpu.roll(row, 2 * LANES - SMAX, 1, stride=1, stride_axis=0)[:, :LANES].astype(BF)
        for half in range(2):
            r = (2 * KPTS + half - lag) % KPTS
            for again in range(2):
                slot = r + KPTS * again
                cols = pl.ds(half * LANES, LANES)
                t_left[rows(slot, SMAX), cols] = block[:SMAX]
                t_main[rows(slot, LANES), cols] = block[SMAX : SMAX + LANES]
                t_right[rows(slot, SMAX), cols] = block[SMAX + LANES :]

    src = lax.broadcasted_iota(jnp.int32, (4 * LANES, 2 * LANES), 0)
    dst = lax.broadcasted_iota(jnp.int32, (4 * LANES, 2 * LANES), 1)
    within = dst % LANES
    wanted = (within // SMAX) * LANES + within % SMAX + (dst // LANES) * (LANES - SMAX)
    pack[...] = (src == wanted).astype(BF)

    prow = lax.broadcasted_iota(jnp.int32, (PAIR, ORB * NB), 0)
    pcol = lax.broadcasted_iota(jnp.int32, (PAIR, ORB * NB), 1)
    for n in range(NB):
        ups[n, 0] = ((prow // ORB) * NB + n == pcol).astype(BF)
        ups[n, 1] = ((prow % ORB) * NB + n == pcol).astype(BF)
    qrow = lax.broadcasted_iota(jnp.int32, (ORB, PAIR), 0)
    qcol = lax.broadcasted_iota(jnp.int32, (ORB, PAIR), 1)
    across_major = (qcol // ORB == qrow).astype(BF)
    across_minor = (qcol % ORB == qrow).astype(BF)

    @pl.loop(0, 8)
    def _(a):
        products = []
        steps_to = []
        blocks = coupling[a].reshape(ORB * NB, ORB)
        wide_major = jnp.dot(blocks, across_major, preferred_element_type=F32).astype(BF)
        wide_minor = jnp.dot(blocks, across_minor, preferred_element_type=F32).astype(BF)
        for n in range(NB):
            first = jnp.dot(ups[n, 0], wide_major, preferred_element_type=F32)
            second = jnp.dot(ups[n, 1], wide_minor, preferred_element_type=F32)
            products.append(first * second)
            steps_to.append(near[a, n] - y * 8 + REACH)
        for table, first_atom in ((k_outer, 8 * (a // 4)), (k_inner, 4)):
            parts = []
            for w in range(4):
                total = jnp.zeros((PAIR, PAIR), F32)
                for n in range(NB):
                    total = total + products[n] * (steps_to[n] == first_atom + w).astype(F32)
                parts.append(total)
            table[rows(a), :] = jnp.concatenate(parts, axis=1).astype(BF)

    @pl.when(head)
    def _():
        for side in sides:
            pl.semaphore_signal(sides_in, inc=1, device_id=side, device_id_type=MESH)
        pl.semaphore_wait(sides_in, len(sides))
        for t, u in steps:
            m_to, zl_to = partner(t, u)
            pl.semaphore_signal(told, inc=1, device_id=at(m_to, zl_to), device_id_type=MESH)

    @pl.when(jnp.logical_not(head))
    def _():
        pl.semaphore_wait(told, 1)

    keep_left = (x > 0).astype(F32)
    keep_right = (x < 3).astype(F32)

    def edge_copies(chunk, t):
        group, _ = partner(t, 0)
        to_left = pltpu.make_async_remote_copy(
            src_ref=left_out.at[chunk, group], dst_ref=right.at[chunk, group, pl.ds(PAIR, PAIR), :],
            send_sem=x_send.at[chunk, t, 0], recv_sem=x_recv.at[chunk, t, 0],
            device_id=x_left, device_id_type=MESH,
        )
        to_right = pltpu.make_async_remote_copy(
            src_ref=right_out.at[chunk, group], dst_ref=left.at[chunk, group, pl.ds(0, PAIR), :],
            send_sem=x_send.at[chunk, t, 1], recv_sem=x_recv.at[chunk, t, 1],
            device_id=x_right, device_id_type=MESH,
        )
        return to_left, to_right

    def home(chunk):
        return outer.at[:, zl, m + REACH] if chunk == 0 else inner.at[:, zl, m]

    def send_out(chunk, t, u):
        m_to, zl_to = partner(t, u)
        return pltpu.make_async_remote_copy(
            src_ref=made.at[chunk, pl.ds(m_to * 4, 4), rows(zl_to), :],
            dst_ref=home(chunk),
            send_sem=out_send.at[chunk, t, u],
            recv_sem=out_recv.at[chunk, t, u],
            device_id=at(m_to, zl_to),
            device_id_type=MESH,
        )

    def own_out(chunk):
        return pltpu.make_async_copy(
            made.at[chunk, pl.ds(m * 4, 4), rows(zl), :], home(chunk), out_local.at[chunk]
        )

    def landed(chunk, part):
        if part == 1:
            for t in range(4):
                send_out(chunk, t, 1).wait_recv()
        else:
            for t in range(3):
                send_out(chunk, t, 0).wait_recv()
            own_out(chunk).wait()

    def c_of(part):
        return 1 - zl if part else zl

    def y_copies(part):
        c = c_of(part)
        down = pltpu.make_async_remote_copy(
            src_ref=outer.at[:, c, pl.ds(2, 2)], dst_ref=outer.at[:, c, pl.ds(6, 2)],
            send_sem=y_send.at[part, 0], recv_sem=y_recv.at[part, 0], device_id=y_left, device_id_type=MESH,
        )
        up = pltpu.make_async_remote_copy(
            src_ref=outer.at[:, c, pl.ds(4, 2)], dst_ref=outer.at[:, c, pl.ds(0, 2)],
            send_sem=y_send.at[part, 1], recv_sem=y_recv.at[part, 1], device_id=y_right, device_id_type=MESH,
        )
        return down, up

    def spread(part):
        landed(0, part)
        for copy in y_copies(part):
            copy.start()

    for chunk in range(2):
        for t in range(4):
            if t < 3:
                send_in(chunk, t, 0).wait_recv()
            else:
                own_in(chunk).wait()
            send_in(chunk, t, 1).wait_recv()
            group, _ = partner(t, 0)
            four = jnp.concatenate([arrived[chunk, group * 4 + i] for i in range(4)], axis=1)
            packed = jnp.dot(four, pack[...], preferred_element_type=F32)
            left_out[chunk, group] = (packed[:PAIR, :LANES] * keep_left).astype(BF)
            left[chunk, group, PAIR:, :] = packed[:PAIR, LANES:].astype(BF)
            right[chunk, group, :PAIR, :] = packed[PAIR:, :LANES].astype(BF)
            right_out[chunk, group] = (packed[PAIR:, LANES:] * keep_right).astype(BF)
            for copy in edge_copies(chunk, t):
                copy.start()
        for t in range(4):
            for copy in edge_copies(chunk, t):
                copy.wait()

        @pl.loop(0, 8)
        def _(turn):
            half, t = turn % 2, turn // 2
            m_to, _ = partner(t, 0)
            kp = m_to * 2 + half
            start = KPTS - 2 * kp
            main = jnp.concatenate([arrived[chunk, q] for q in range(KPTS)], axis=1)
            total = jnp.dot(
                main, t_main[pl.ds(pl.multiple_of(start * LANES, LANES), KPTS * LANES), :],
                preferred_element_type=F32,
            )
            window = pl.ds(pl.multiple_of(start * SMAX, SMAX), KPTS * SMAX)
            lows = jnp.concatenate([left[chunk, g] for g in range(4)], axis=1)
            total = total + jnp.dot(lows, t_left[window, :], preferred_element_type=F32)
            highs = jnp.concatenate([right[chunk, g] for g in range(4)], axis=1)
            total = total + jnp.dot(highs, t_right[window, :], preferred_element_type=F32)
            total = total.astype(BF)
            made[chunk, 2 * kp] = total[:, :LANES]
            made[chunk, 2 * kp + 1] = total[:, LANES:]

            @pl.when((half == 1) & (t < 3))
            def _():
                send_out(chunk, t, 0).start()

            @pl.when(turn == 7)
            def _():
                own_out(chunk).start()
                for near_t in range(4):
                    send_out(chunk, near_t, 1).start()

            if chunk == 1:

                @pl.when(turn == 1)
                def _():
                    spread(0)

    spread(1)

    def pair_of(source, half, c, first):
        two = [source[2 * half + j, c, pl.ds(first, 4)].reshape(4 * PAIR, LANES) for j in range(2)]
        return jnp.concatenate(two, axis=1)

    def apply_outer(half, part):
        if half == 0:
            for copy in y_copies(part):
                copy.wait()
        c = c_of(part)

        @pl.loop(0, 2)
        def _(side):
            operand = pair_of(outer, half, c, 4 * side)
            for part in range(2):
                a = 4 * side + 2 * part
                block = jnp.dot(k_outer[rows(2 * side + part, 2 * PAIR), :], operand, preferred_element_type=F32)
                for i in range(2):
                    for j in range(2):
                        out[2 * half + j, a + i, c] = block[i * PAIR : (i + 1) * PAIR, j * LANES : (j + 1) * LANES]

    def apply_inner(half, part):
        if half == 0:
            landed(1, part)
        c = c_of(part)

        @pl.loop(0, 2)
        def _(side):
            operand = pair_of(inner, half, c, 0)
            for part in range(2):
                a = 4 * side + 2 * part
                block = jnp.dot(k_inner[rows(2 * side + part, 2 * PAIR), :], operand, preferred_element_type=F32)
                for i in range(2):
                    for j in range(2):
                        out[2 * half + j, a + i, c] += block[i * PAIR : (i + 1) * PAIR, j * LANES : (j + 1) * LANES]

    for half in range(2):
        apply_outer(half, 0)
    for half in range(2):
        apply_inner(half, 0)
    for half in range(2):
        apply_outer(half, 1)
    landed(1, 1)
    for chunk in range(2):
        for t, u in steps:
            send_in(chunk, t, u).wait_send()
    for chunk in range(2):
        for t, u in steps:
            send_out(chunk, t, u).wait_send()


def finish_kernel(most, last, k_inner, out, block, sems):
    c = 1 - lax.axis_index("energy") % 2
    copies = [pltpu.make_async_copy(most.at[:, :, 1 - c], out.at[:, :, 1 - c], sems.at[0])]
    copies[0].start()
    for half in range(2):
        operand = jnp.concatenate([last[2 * half + j, c].reshape(4 * PAIR, LANES) for j in range(2)], axis=1)
        for side in range(2):
            for part in range(2):
                a = 4 * side + 2 * part
                product = jnp.dot(k_inner[a * PAIR : (a + 2) * PAIR, :], operand, preferred_element_type=F32)
                for i in range(2):
                    for j in range(2):
                        k = 2 * half + j
                        block[k, a + i] = most[k, a + i, c] + product[i * PAIR : (i + 1) * PAIR, j * LANES : (j + 1) * LANES]
            ks, atoms = pl.ds(2 * half, 2), pl.ds(4 * side, 4)
            copy = pltpu.make_async_copy(block.at[ks, atoms], out.at[ks, atoms, c], sems.at[1 + 2 * half + side])
            copy.start()
            copies.append(copy)
    for copy in copies:
        copy.wait()


def shards(green, neighbours, offsets, emit_weight, absorb_weight, coupling):
    k_count, a_count, components, e_count = green.shape
    hbm = pl.BlockSpec(memory_space=pltpu.HBM)
    dma = pltpu.SemaphoreType.DMA
    regular = pltpu.SemaphoreType.REGULAR
    vmem = pltpu.VMEM
    shape = jax.ShapeDtypeStruct((k_count, a_count, 2, PAIR, e_count), F32)
    in_vmem = pl.BlockSpec(memory_space=vmem)
    most, last, k_inner = pl.pallas_call(
        exchange_kernel,
        out_shape=(
            shape,
            jax.ShapeDtypeStruct((k_count, 2, 4, PAIR, LANES), BF),
            jax.ShapeDtypeStruct((a_count * PAIR, 4 * PAIR), BF),
        ),
        in_specs=[hbm] * 6,
        out_specs=(in_vmem,) * 3,
        scratch_shapes=[
            vmem((2, KPTS, 2 * PAIR, LANES), BF),
            vmem((2, KPTS, 2 * PAIR, LANES), BF),
            vmem((2, 4, 2 * PAIR, LANES), BF),
            vmem((2, 4, 2 * PAIR, LANES), BF),
            vmem((2, 4, PAIR, LANES), BF),
            vmem((2, 4, PAIR, LANES), BF),
            vmem((k_count, 2, 8, PAIR, LANES), BF),
            vmem((KPTS, 2 * LANES), F32),
            vmem((2 * KPTS * LANES, 2 * LANES), BF),
            vmem((2 * KPTS * SMAX, 2 * LANES), BF),
            vmem((2 * KPTS * SMAX, 2 * LANES), BF),
            vmem((4 * LANES, 2 * LANES), BF),
            vmem((a_count * PAIR, 4 * PAIR), BF),
            pltpu.SMEM((a_count, NB), jnp.int32),
            pltpu.SMEM((KPTS,), jnp.int32),
            vmem((KPTS, KPTS), BF),
            vmem((KPTS, KPTS), BF),
            vmem((a_count, ORB, NB, ORB), BF),
            vmem((NB, 2, PAIR, ORB * NB), BF),
            vmem((k_count, a_count, 2, PAIR, LANES), BF),
            dma((2, 4, 2)), dma((2, 4, 2)), dma((2,)),
            dma((2, 4, 2)), dma((2, 4, 2)),
            dma((2, 4, 2)), dma((2, 4, 2)), dma((2,)),
            dma((2, 2)), dma((2, 2)), dma((6,)),
            regular, regular,
        ],
        compiler_params=pltpu.CompilerParams(
            collective_id=0, has_side_effects=True, vmem_limit_bytes=40 * 1024 * 1024
        ),
        name="exchange",
    )(
        *(
            pltpu.with_memory_space_constraint(array, pltpu.HBM)
            for array in (
                green.reshape(k_count, a_count, 2, PAIR, e_count),
                neighbours,
                offsets,
                emit_weight,
                absorb_weight,
                coupling.transpose(0, 2, 1, 3),
            )
        )
    )
    out = pl.pallas_call(
        finish_kernel,
        out_shape=shape,
        in_specs=[in_vmem] * 3,
        out_specs=hbm,
        scratch_shapes=[vmem((k_count, a_count, PAIR, LANES), F32), dma((5,))],
        compiler_params=pltpu.CompilerParams(vmem_limit_bytes=8 * 1024 * 1024),
        name="finish",
    )(most, last, k_inner)
    return out.reshape(k_count, a_count, components, e_count)


def solution(mesh):
    in_specs = (
        P("momentum", "atom", None, "energy"),
        P("atom", None),
        P(),
        P(),
        P(),
        P("atom", None, None, None),
    )
    out_specs = P("momentum", "atom", None, "energy")
    return jax.shard_map(shards, mesh=mesh, in_specs=in_specs, out_specs=out_specs, check_vma=False)
```

```python
import functools

import jax
import jax.numpy as jnp
from jax import lax
from jax.experimental import pallas as pl
from jax.experimental.pallas import tpu as pltpu
from jax.sharding import PartitionSpec as P

ORB = 12
NB = 8
SMAX = 32
REACH = 2
KPTS = 16
PAIR = ORB * ORB
LANES = 128
SPAN = 2 * REACH + 1
MESH = pl.DeviceIdType.MESH
BF = jnp.bfloat16
F32 = jnp.float32


def place():
    e = lax.axis_index("energy")
    m = lax.axis_index("momentum")
    return e // 2, e % 2, m // 2, m % 2


def partner(t, u):
    _, zl, zh, core = place()
    far = 1 - t // 2
    flip = ((t + 1) // 2) % 2
    zh_t = zh + far * (1 - 2 * zh)
    core_t = core + flip * (1 - 2 * core)
    zl_t = zl + u * (1 - 2 * zl)
    return zh_t * 2 + core_t, zl_t


def share(chunk, m, zl):
    if chunk == 0:
        return m + 4 * (m // 2), zl
    return m + 2, zl


def exchange_kernel(
    green_hbm, near_hbm, offsets_hbm, emit_hbm, absorb_hbm, coupling_hbm,
    out, inner, k_inner,
    arrived, made, left, right, left_out, right_out, outer,
    base, t_main, t_left, t_right, pack, k_outer,
    near, offsets, emit, absorb, coupling, ups, green,
    in_send, in_recv, in_local, x_send, x_recv, out_send, out_recv, out_local, y_send, y_recv, small,
    sides_in, told,
):
    x, zl, zh, core = place()
    m = zh * 2 + core
    y = lax.axis_index("atom")

    def at(m_to, zl_to):
        return {"energy": x * 2 + zl_to, "momentum": m_to}

    x_left = {"energy": ((x + 3) % 4) * 2 + zl}
    x_right = {"energy": ((x + 1) % 4) * 2 + zl}
    y_left = {"atom": (y + 3) % 4}
    y_right = {"atom": (y + 1) % 4}

    barrier = pltpu.get_barrier_semaphore()
    steps = [(t, u) for t in range(4) for u in range(2) if (t, u) != (3, 0)]
    prefetch = pltpu.make_async_copy(green_hbm, green, small.at[5])
    prefetch.start()
    sides = (x_left, x_right, y_left, y_right)
    head = m * 2 + zl == 0
    for t, u in steps:
        m_to, zl_to = partner(t, u)
        pl.semaphore_signal(barrier, inc=1, device_id=at(m_to, zl_to), device_id_type=MESH)

    @pl.when(head)
    def _():
        for side in sides:
            pl.semaphore_signal(barrier, inc=1, device_id=side, device_id_type=MESH)

    fetches = [
        pltpu.make_async_copy(src, dst, small.at[i])
        for i, (src, dst) in enumerate(
            ((near_hbm, near), (offsets_hbm, offsets), (emit_hbm, emit), (absorb_hbm, absorb), (coupling_hbm, coupling))
        )
    ]
    for copy in fetches:
        copy.start()
    prefetch.wait()
    pl.semaphore_wait(barrier, len(steps) + len(sides) * head.astype(jnp.int32))


    def rows(block, count=PAIR):
        return pl.ds(pl.multiple_of(block * count, 16), count)

    def send_in(chunk, t, u):
        m_to, zl_to = partner(t, u)
        atom, c = share(chunk, m_to, zl_to)
        return pltpu.make_async_remote_copy(
            src_ref=green.at[:, atom, c],
            dst_ref=arrived.at[chunk, pl.ds(m * 4, 4), rows(zl), :],
            send_sem=in_send.at[chunk, t, u],
            recv_sem=in_recv.at[chunk, t, u],
            device_id=at(m_to, zl_to),
            device_id_type=MESH,
        )

    def own_in(chunk):
        atom, c = share(chunk, m, zl)
        return pltpu.make_async_copy(
            green.at[:, atom, c], arrived.at[chunk, pl.ds(m * 4, 4), rows(zl), :], in_local.at[chunk]
        )

    for chunk in range(2):
        for t, u in ((0, 0), (3, 1), (0, 1), (1, 0), (2, 1), (1, 1), (2, 0)):
            send_in(chunk, t, u).start()
        own_in(chunk).start()
    for copy in fetches:
        copy.wait()

    lane = lax.broadcasted_iota(jnp.int32, (KPTS, 2 * LANES), 1)
    line = lax.broadcasted_iota(jnp.int32, (KPTS, 2 * LANES), 0)
    shift = jnp.zeros((KPTS, 2 * LANES), jnp.int32)
    for w in range(KPTS):
        shift = jnp.where(line == w, offsets[w], shift)
    emit_pick = (lane == shift).astype(BF)
    absorb_pick = (lane == 2 * LANES - shift).astype(BF)
    dims = (((0,), (0,)), ((), ()))
    base[...] = lax.dot_general(emit[...], emit_pick, dims, preferred_element_type=F32) + lax.dot_general(
        absorb[...], absorb_pick, dims, preferred_element_type=F32
    )
    span = LANES + 2 * SMAX

    @pl.loop(0, KPTS)
    def _(lag):
        row = jnp.broadcast_to(base[pl.ds(lag, 1), :], (span, 2 * LANES))
        block = pltpu.roll(row, 2 * LANES - SMAX, 1, stride=1, stride_axis=0)[:, :LANES].astype(BF)
        for half in range(2):
            r = (2 * KPTS + half - lag) % KPTS
            for again in range(2):
                slot = r + KPTS * again
                cols = pl.ds(half * LANES, LANES)
                t_left[rows(slot, SMAX), cols] = block[:SMAX]
                t_main[rows(slot, LANES), cols] = block[SMAX : SMAX + LANES]
                t_right[rows(slot, SMAX), cols] = block[SMAX + LANES :]

    src = lax.broadcasted_iota(jnp.int32, (4 * LANES, 2 * LANES), 0)
    dst = lax.broadcasted_iota(jnp.int32, (4 * LANES, 2 * LANES), 1)
    within = dst % LANES
    wanted = (within // SMAX) * LANES + within % SMAX + (dst // LANES) * (LANES - SMAX)
    pack[...] = (src == wanted).astype(BF)

    prow = lax.broadcasted_iota(jnp.int32, (PAIR, ORB * NB), 0)
    pcol = lax.broadcasted_iota(jnp.int32, (PAIR, ORB * NB), 1)
    for n in range(NB):
        ups[n, 0] = ((prow // ORB) * NB + n == pcol).astype(BF)
        ups[n, 1] = ((prow % ORB) * NB + n == pcol).astype(BF)
    qrow = lax.broadcasted_iota(jnp.int32, (ORB, PAIR), 0)
    qcol = lax.broadcasted_iota(jnp.int32, (ORB, PAIR), 1)
    across_major = (qcol // ORB == qrow).astype(BF)
    across_minor = (qcol % ORB == qrow).astype(BF)

    @pl.loop(0, 8)
    def _(a):
        products = []
        steps_to = []
        blocks = coupling[a].reshape(ORB * NB, ORB)
        wide_major = jnp.dot(blocks, across_major, preferred_element_type=F32).astype(BF)
        wide_minor = jnp.dot(blocks, across_minor, preferred_element_type=F32).astype(BF)
        for n in range(NB):
            first = jnp.dot(ups[n, 0], wide_major, preferred_element_type=F32)
            second = jnp.dot(ups[n, 1], wide_minor, preferred_element_type=F32)
            products.append(first * second)
            steps_to.append(near[a, n] - y * 8 + REACH)
        for table, first_atom in ((k_outer, 8 * (a // 4)), (k_inner, 4)):
            parts = []
            for w in range(4):
                total = jnp.zeros((PAIR, PAIR), F32)
                for n in range(NB):
                    total = total + products[n] * (steps_to[n] == first_atom + w).astype(F32)
                parts.append(total)
            table[rows(a), :] = jnp.concatenate(parts, axis=1).astype(BF)

    @pl.when(head)
    def _():
        for side in sides:
            pl.semaphore_signal(sides_in, inc=1, device_id=side, device_id_type=MESH)
        pl.semaphore_wait(sides_in, len(sides))
        for t, u in steps:
            m_to, zl_to = partner(t, u)
            pl.semaphore_signal(told, inc=1, device_id=at(m_to, zl_to), device_id_type=MESH)

    @pl.when(jnp.logical_not(head))
    def _():
        pl.semaphore_wait(told, 1)

    keep_left = (x > 0).astype(F32)
    keep_right = (x < 3).astype(F32)

    def edge_copies(chunk, t):
        group, _ = partner(t, 0)
        to_left = pltpu.make_async_remote_copy(
            src_ref=left_out.at[chunk, group], dst_ref=right.at[chunk, group, pl.ds(PAIR, PAIR), :],
            send_sem=x_send.at[chunk, t, 0], recv_sem=x_recv.at[chunk, t, 0],
            device_id=x_left, device_id_type=MESH,
        )
        to_right = pltpu.make_async_remote_copy(
            src_ref=right_out.at[chunk, group], dst_ref=left.at[chunk, group, pl.ds(0, PAIR), :],
            send_sem=x_send.at[chunk, t, 1], recv_sem=x_recv.at[chunk, t, 1],
            device_id=x_right, device_id_type=MESH,
        )
        return to_left, to_right

    def home(chunk, half):
        ks = pl.ds(2 * half, 2)
        return outer.at[ks, zl, m + REACH] if chunk == 0 else inner.at[ks, zl, m]

    def send_out(chunk, half, t, u):
        m_to, zl_to = partner(t, u)
        return pltpu.make_async_remote_copy(
            src_ref=made.at[chunk, pl.ds(m_to * 4 + 2 * half, 2), rows(zl_to), :],
            dst_ref=home(chunk, half),
            send_sem=out_send.at[chunk, half, t, u],
            recv_sem=out_recv.at[chunk, half, t, u],
            device_id=at(m_to, zl_to),
            device_id_type=MESH,
        )

    def own_out(chunk, half):
        return pltpu.make_async_copy(
            made.at[chunk, pl.ds(m * 4 + 2 * half, 2), rows(zl), :], home(chunk, half), out_local.at[chunk, half]
        )

    def landed(chunk, half, part):
        if part == 1:
            for t in range(4):
                send_out(chunk, half, t, 1).wait_recv()
        else:
            for t in range(3):
                send_out(chunk, half, t, 0).wait_recv()
            own_out(chunk, half).wait()

    def c_of(part):
        return 1 - zl if part else zl

    def y_copies(half, part):
        ks, c = pl.ds(2 * half, 2), c_of(part)
        down = pltpu.make_async_remote_copy(
            src_ref=outer.at[ks, c, pl.ds(2, 2)], dst_ref=outer.at[ks, c, pl.ds(6, 2)],
            send_sem=y_send.at[half, part, 0], recv_sem=y_recv.at[half, part, 0],
            device_id=y_left, device_id_type=MESH,
        )
        up = pltpu.make_async_remote_copy(
            src_ref=outer.at[ks, c, pl.ds(4, 2)], dst_ref=outer.at[ks, c, pl.ds(0, 2)],
            send_sem=y_send.at[half, part, 1], recv_sem=y_recv.at[half, part, 1],
            device_id=y_right, device_id_type=MESH,
        )
        return down, up

    def spread(half, part):
        landed(0, half, part)
        for copy in y_copies(half, part):
            copy.start()

    for chunk in range(2):
        for t in range(4):
            if t < 3:
                send_in(chunk, t, 0).wait_recv()
            else:
                own_in(chunk).wait()
            send_in(chunk, t, 1).wait_recv()
            group, _ = partner(t, 0)
            four = jnp.concatenate([arrived[chunk, group * 4 + i] for i in range(4)], axis=1)
            packed = jnp.dot(four, pack[...], preferred_element_type=F32)
            left_out[chunk, group] = (packed[:PAIR, :LANES] * keep_left).astype(BF)
            left[chunk, group, PAIR:, :] = packed[:PAIR, LANES:].astype(BF)
            right[chunk, group, :PAIR, :] = packed[PAIR:, :LANES].astype(BF)
            right_out[chunk, group] = (packed[PAIR:, LANES:] * keep_right).astype(BF)
            for copy in edge_copies(chunk, t):
                copy.start()
        if chunk == 1:
            spread(0, 0)
        for t in range(4):
            for copy in edge_copies(chunk, t):
                copy.wait()

        @pl.loop(0, 8)
        def _(turn):
            half, t = turn // 4, turn % 4
            m_to, _ = partner(t, 0)
            kp = m_to * 2 + half
            start = KPTS - 2 * kp
            main = jnp.concatenate([arrived[chunk, q] for q in range(KPTS)], axis=1)
            total = jnp.dot(
                main, t_main[pl.ds(pl.multiple_of(start * LANES, LANES), KPTS * LANES), :],
                preferred_element_type=F32,
            )
            window = pl.ds(pl.multiple_of(start * SMAX, SMAX), KPTS * SMAX)
            lows = jnp.concatenate([left[chunk, g] for g in range(4)], axis=1)
            total = total + jnp.dot(lows, t_left[window, :], preferred_element_type=F32)
            highs = jnp.concatenate([right[chunk, g] for g in range(4)], axis=1)
            total = total + jnp.dot(highs, t_right[window, :], preferred_element_type=F32)
            total = total.astype(BF)
            made[chunk, 2 * kp] = total[:, :LANES]
            made[chunk, 2 * kp + 1] = total[:, LANES:]

            @pl.when(t < 3)
            def _():
                send_out(chunk, half, t, 0).start()

            @pl.when(t == 3)
            def _():
                own_out(chunk, half).start()
                for near_t in range(4):
                    send_out(chunk, half, near_t, 1).start()

            if chunk == 1:

                @pl.when(turn == 0)
                def _():
                    spread(0, 1)

                @pl.when(turn == 5)
                def _():
                    spread(1, 0)

    spread(1, 1)

    def pair_of(source, half, c, first):
        two = [source[2 * half + j, c, pl.ds(first, 4)].reshape(4 * PAIR, LANES) for j in range(2)]
        return jnp.concatenate(two, axis=1)

    def apply_outer(half, part):
        for copy in y_copies(half, part):
            copy.wait()
        c = c_of(part)

        @pl.loop(0, 2)
        def _(side):
            operand = pair_of(outer, half, c, 4 * side)
            for part in range(2):
                a = 4 * side + 2 * part
                block = jnp.dot(k_outer[rows(2 * side + part, 2 * PAIR), :], operand, preferred_element_type=F32)
                for i in range(2):
                    for j in range(2):
                        out[2 * half + j, a + i, c] = block[i * PAIR : (i + 1) * PAIR, j * LANES : (j + 1) * LANES]

    def apply_inner(half, part):
        landed(1, half, part)
        c = c_of(part)

        @pl.loop(0, 2)
        def _(side):
            operand = pair_of(inner, half, c, 0)
            for part in range(2):
                a = 4 * side + 2 * part
                block = jnp.dot(k_inner[rows(2 * side + part, 2 * PAIR), :], operand, preferred_element_type=F32)
                for i in range(2):
                    for j in range(2):
                        out[2 * half + j, a + i, c] += block[i * PAIR : (i + 1) * PAIR, j * LANES : (j + 1) * LANES]

    apply_outer(0, 0)
    apply_outer(0, 1)
    apply_inner(0, 0)
    apply_outer(1, 0)
    apply_inner(0, 1)
    apply_outer(1, 1)
    apply_inner(1, 0)
    landed(1, 1, 1)
    for chunk in range(2):
        for t, u in steps:
            send_in(chunk, t, u).wait_send()
    for chunk in range(2):
        for half in range(2):
            for t, u in steps:
                send_out(chunk, half, t, u).wait_send()


def finish_kernel(most, last, k_inner, out, block, sems):
    c = 1 - lax.axis_index("energy") % 2
    second = pl.ds(2, 2)
    copies = [
        pltpu.make_async_copy(most.at[0], out.at[0], sems.at[0]),
        pltpu.make_async_copy(most.at[1], out.at[1], sems.at[4]),
        pltpu.make_async_copy(most.at[2, :, 1 - c], out.at[2, :, 1 - c], sems.at[1]),
        pltpu.make_async_copy(most.at[3, :, 1 - c], out.at[3, :, 1 - c], sems.at[5]),
    ]
    for copy in copies:
        copy.start()
    operand = jnp.concatenate([last[2 + j, c].reshape(4 * PAIR, LANES) for j in range(2)], axis=1)
    for side in range(2):
        for part in range(2):
            a = 4 * side + 2 * part
            product = jnp.dot(k_inner[a * PAIR : (a + 2) * PAIR, :], operand, preferred_element_type=F32)
            for i in range(2):
                for j in range(2):
                    block[j, a + i] = most[2 + j, a + i, c] + product[i * PAIR : (i + 1) * PAIR, j * LANES : (j + 1) * LANES]
        atoms = pl.ds(4 * side, 4)
        copy = pltpu.make_async_copy(block.at[:, atoms], out.at[second, atoms, c], sems.at[2 + side])
        copy.start()
        copies.append(copy)
    for copy in copies:
        copy.wait()


def shards(green, neighbours, offsets, emit_weight, absorb_weight, coupling):
    k_count, a_count, components, e_count = green.shape
    hbm = pl.BlockSpec(memory_space=pltpu.HBM)
    dma = pltpu.SemaphoreType.DMA
    regular = pltpu.SemaphoreType.REGULAR
    vmem = pltpu.VMEM
    shape = jax.ShapeDtypeStruct((k_count, a_count, 2, PAIR, e_count), F32)
    in_vmem = pl.BlockSpec(memory_space=vmem)
    most, last, k_inner = pl.pallas_call(
        exchange_kernel,
        out_shape=(
            shape,
            jax.ShapeDtypeStruct((k_count, 2, 4, PAIR, LANES), BF),
            jax.ShapeDtypeStruct((a_count * PAIR, 4 * PAIR), BF),
        ),
        in_specs=[hbm] * 6,
        out_specs=(in_vmem,) * 3,
        scratch_shapes=[
            vmem((2, KPTS, 2 * PAIR, LANES), BF),
            vmem((2, KPTS, 2 * PAIR, LANES), BF),
            vmem((2, 4, 2 * PAIR, LANES), BF),
            vmem((2, 4, 2 * PAIR, LANES), BF),
            vmem((2, 4, PAIR, LANES), BF),
            vmem((2, 4, PAIR, LANES), BF),
            vmem((k_count, 2, 8, PAIR, LANES), BF),
            vmem((KPTS, 2 * LANES), F32),
            vmem((2 * KPTS * LANES, 2 * LANES), BF),
            vmem((2 * KPTS * SMAX, 2 * LANES), BF),
            vmem((2 * KPTS * SMAX, 2 * LANES), BF),
            vmem((4 * LANES, 2 * LANES), BF),
            vmem((a_count * PAIR, 4 * PAIR), BF),
            pltpu.SMEM((a_count, NB), jnp.int32),
            pltpu.SMEM((KPTS,), jnp.int32),
            vmem((KPTS, KPTS), BF),
            vmem((KPTS, KPTS), BF),
            vmem((a_count, ORB, NB, ORB), BF),
            vmem((NB, 2, PAIR, ORB * NB), BF),
            vmem((k_count, a_count, 2, PAIR, LANES), BF),
            dma((2, 4, 2)), dma((2, 4, 2)), dma((2,)),
            dma((2, 4, 2)), dma((2, 4, 2)),
            dma((2, 2, 4, 2)), dma((2, 2, 4, 2)), dma((2, 2)),
            dma((2, 2, 2)), dma((2, 2, 2)), dma((6,)),
            regular, regular,
        ],
        compiler_params=pltpu.CompilerParams(
            collective_id=0, has_side_effects=True, vmem_limit_bytes=40 * 1024 * 1024
        ),
        name="exchange",
    )(
        *(
            pltpu.with_memory_space_constraint(array, pltpu.HBM)
            for array in (
                green.reshape(k_count, a_count, 2, PAIR, e_count),
                neighbours,
                offsets,
                emit_weight,
                absorb_weight,
                coupling.transpose(0, 2, 1, 3),
            )
        )
    )
    out = pl.pallas_call(
        finish_kernel,
        out_shape=shape,
        in_specs=[in_vmem] * 3,
        out_specs=hbm,
        scratch_shapes=[vmem((2, a_count, PAIR, LANES), F32), dma((6,))],
        compiler_params=pltpu.CompilerParams(vmem_limit_bytes=8 * 1024 * 1024),
        name="finish",
    )(most, last, k_inner)
    return out.reshape(k_count, a_count, components, e_count)


def solution(mesh):
    in_specs = (
        P("momentum", "atom", None, "energy"),
        P("atom", None),
        P(),
        P(),
        P(),
        P("atom", None, None, None),
    )
    out_specs = P("momentum", "atom", None, "energy")
    return jax.shard_map(shards, mesh=mesh, in_specs=in_specs, out_specs=out_specs, check_vma=False)
```

```python
import functools

import jax
import jax.numpy as jnp
from jax import lax
from jax.experimental import pallas as pl
from jax.experimental.pallas import tpu as pltpu
from jax.sharding import PartitionSpec as P

ORB = 12
NB = 8
SMAX = 32
REACH = 2
KPTS = 16
PAIR = ORB * ORB
LANES = 128
SPAN = 2 * REACH + 1
MESH = pl.DeviceIdType.MESH
BF = jnp.bfloat16
F32 = jnp.float32


def place():
    e = lax.axis_index("energy")
    m = lax.axis_index("momentum")
    return e // 2, e % 2, m // 2, m % 2


def partner(t, u):
    _, zl, zh, core = place()
    far = 1 - t // 2
    flip = ((t + 1) // 2) % 2
    zh_t = zh + far * (1 - 2 * zh)
    core_t = core + flip * (1 - 2 * core)
    zl_t = zl + u * (1 - 2 * zl)
    return zh_t * 2 + core_t, zl_t


def share(chunk, m, zl):
    if chunk == 0:
        return m + 4 * (m // 2), zl
    return m + 2, zl


def exchange_kernel(
    green_hbm, near_hbm, offsets_hbm, emit_hbm, absorb_hbm, coupling_hbm,
    out, inner, k_inner,
    arrived, made, left, right, left_out, right_out, outer,
    base, t_main, t_left, t_right, pack, k_outer,
    near, offsets, emit, absorb, coupling, ups, green,
    in_send, in_recv, in_local, x_send, x_recv, out_send, out_recv, out_local, y_send, y_recv, small,
    sides_in, told,
):
    x, zl, zh, core = place()
    m = zh * 2 + core
    y = lax.axis_index("atom")

    def at(m_to, zl_to):
        return {"energy": x * 2 + zl_to, "momentum": m_to}

    x_left = {"energy": ((x + 3) % 4) * 2 + zl}
    x_right = {"energy": ((x + 1) % 4) * 2 + zl}
    y_left = {"atom": (y + 3) % 4}
    y_right = {"atom": (y + 1) % 4}

    barrier = pltpu.get_barrier_semaphore()
    steps = [(t, u) for t in range(4) for u in range(2) if (t, u) != (3, 0)]
    sides = (x_left, x_right, y_left, y_right)
    head = m * 2 + zl == 0
    for t, u in steps:
        m_to, zl_to = partner(t, u)
        pl.semaphore_signal(barrier, inc=1, device_id=at(m_to, zl_to), device_id_type=MESH)

    @pl.when(head)
    def _():
        for side in sides:
            pl.semaphore_signal(barrier, inc=1, device_id=side, device_id_type=MESH)

    prefetch = pltpu.make_async_copy(green_hbm, green, small.at[5])
    prefetch.start()
    fetches = [
        pltpu.make_async_copy(src, dst, small.at[i])
        for i, (src, dst) in enumerate(
            ((near_hbm, near), (offsets_hbm, offsets), (emit_hbm, emit), (absorb_hbm, absorb), (coupling_hbm, coupling))
        )
    ]
    for copy in fetches:
        copy.start()
    prefetch.wait()
    pl.semaphore_wait(barrier, len(steps) + len(sides) * head.astype(jnp.int32))


    def rows(block, count=PAIR):
        return pl.ds(pl.multiple_of(block * count, 16), count)

    def send_in(chunk, t, u):
        m_to, zl_to = partner(t, u)
        atom, c = share(chunk, m_to, zl_to)
        return pltpu.make_async_remote_copy(
            src_ref=green.at[:, atom, c],
            dst_ref=arrived.at[chunk, pl.ds(m * 4, 4), rows(zl), :],
            send_sem=in_send.at[chunk, t, u],
            recv_sem=in_recv.at[chunk, t, u],
            device_id=at(m_to, zl_to),
            device_id_type=MESH,
        )

    def own_in(chunk):
        atom, c = share(chunk, m, zl)
        return pltpu.make_async_copy(
            green.at[:, atom, c], arrived.at[chunk, pl.ds(m * 4, 4), rows(zl), :], in_local.at[chunk]
        )

    for chunk in range(2):
        for t, u in steps:
            send_in(chunk, t, u).start()
        own_in(chunk).start()
    for copy in fetches:
        copy.wait()

    lane = lax.broadcasted_iota(jnp.int32, (KPTS, 2 * LANES), 1)
    line = lax.broadcasted_iota(jnp.int32, (KPTS, 2 * LANES), 0)
    shift = jnp.zeros((KPTS, 2 * LANES), jnp.int32)
    for w in range(KPTS):
        shift = jnp.where(line == w, offsets[w], shift)
    emit_pick = (lane == shift).astype(BF)
    absorb_pick = (lane == 2 * LANES - shift).astype(BF)
    dims = (((0,), (0,)), ((), ()))
    base[...] = lax.dot_general(emit[...], emit_pick, dims, preferred_element_type=F32) + lax.dot_general(
        absorb[...], absorb_pick, dims, preferred_element_type=F32
    )
    span = LANES + 2 * SMAX

    @pl.loop(0, KPTS)
    def _(lag):
        row = jnp.broadcast_to(base[pl.ds(lag, 1), :], (span, 2 * LANES))
        block = pltpu.roll(row, 2 * LANES - SMAX, 1, stride=1, stride_axis=0)[:, :LANES].astype(BF)
        for half in range(2):
            r = (2 * KPTS + half - lag) % KPTS
            for again in range(2):
                slot = r + KPTS * again
                cols = pl.ds(half * LANES, LANES)
                t_left[rows(slot, SMAX), cols] = block[:SMAX]
                t_main[rows(slot, LANES), cols] = block[SMAX : SMAX + LANES]
                t_right[rows(slot, SMAX), cols] = block[SMAX + LANES :]

    src = lax.broadcasted_iota(jnp.int32, (4 * LANES, 2 * LANES), 0)
    dst = lax.broadcasted_iota(jnp.int32, (4 * LANES, 2 * LANES), 1)
    within = dst % LANES
    wanted = (within // SMAX) * LANES + within % SMAX + (dst // LANES) * (LANES - SMAX)
    pack[...] = (src == wanted).astype(BF)

    prow = lax.broadcasted_iota(jnp.int32, (PAIR, ORB * NB), 0)
    pcol = lax.broadcasted_iota(jnp.int32, (PAIR, ORB * NB), 1)
    for n in range(NB):
        ups[n, 0] = ((prow // ORB) * NB + n == pcol).astype(BF)
        ups[n, 1] = ((prow % ORB) * NB + n == pcol).astype(BF)
    qrow = lax.broadcasted_iota(jnp.int32, (ORB, PAIR), 0)
    qcol = lax.broadcasted_iota(jnp.int32, (ORB, PAIR), 1)
    across_major = (qcol // ORB == qrow).astype(BF)
    across_minor = (qcol % ORB == qrow).astype(BF)

    @pl.loop(0, 8)
    def _(a):
        products = []
        steps_to = []
        blocks = coupling[a].reshape(ORB * NB, ORB)
        wide_major = jnp.dot(blocks, across_major, preferred_element_type=F32).astype(BF)
        wide_minor = jnp.dot(blocks, across_minor, preferred_element_type=F32).astype(BF)
        for n in range(NB):
            first = jnp.dot(ups[n, 0], wide_major, preferred_element_type=F32)
            second = jnp.dot(ups[n, 1], wide_minor, preferred_element_type=F32)
            products.append(first * second)
            steps_to.append(near[a, n] - y * 8 + REACH)
        for table, first_atom in ((k_outer, 8 * (a // 4)), (k_inner, 4)):
            parts = []
            for w in range(4):
                total = jnp.zeros((PAIR, PAIR), F32)
                for n in range(NB):
                    total = total + products[n] * (steps_to[n] == first_atom + w).astype(F32)
                parts.append(total)
            table[rows(a), :] = jnp.concatenate(parts, axis=1).astype(BF)

    @pl.when(head)
    def _():
        for side in sides:
            pl.semaphore_signal(sides_in, inc=1, device_id=side, device_id_type=MESH)
        pl.semaphore_wait(sides_in, len(sides))
        for t, u in steps:
            m_to, zl_to = partner(t, u)
            pl.semaphore_signal(told, inc=1, device_id=at(m_to, zl_to), device_id_type=MESH)

    @pl.when(jnp.logical_not(head))
    def _():
        pl.semaphore_wait(told, 1)

    keep_left = (x > 0).astype(F32)
    keep_right = (x < 3).astype(F32)

    def edge_copies(chunk, t):
        group, _ = partner(t, 0)
        to_left = pltpu.make_async_remote_copy(
            src_ref=left_out.at[chunk, group], dst_ref=right.at[chunk, group, pl.ds(PAIR, PAIR), :],
            send_sem=x_send.at[chunk, t, 0], recv_sem=x_recv.at[chunk, t, 0],
            device_id=x_left, device_id_type=MESH,
        )
        to_right = pltpu.make_async_remote_copy(
            src_ref=right_out.at[chunk, group], dst_ref=left.at[chunk, group, pl.ds(0, PAIR), :],
            send_sem=x_send.at[chunk, t, 1], recv_sem=x_recv.at[chunk, t, 1],
            device_id=x_right, device_id_type=MESH,
        )
        return to_left, to_right

    def home(chunk, half):
        ks = pl.ds(2 * half, 2)
        return outer.at[ks, zl, m + REACH] if chunk == 0 else inner.at[ks, zl, m]

    def send_out(chunk, half, t, u):
        m_to, zl_to = partner(t, u)
        return pltpu.make_async_remote_copy(
            src_ref=made.at[chunk, pl.ds(m_to * 4 + 2 * half, 2), rows(zl_to), :],
            dst_ref=home(chunk, half),
            send_sem=out_send.at[chunk, half, t, u],
            recv_sem=out_recv.at[chunk, half, t, u],
            device_id=at(m_to, zl_to),
            device_id_type=MESH,
        )

    def own_out(chunk, half):
        return pltpu.make_async_copy(
            made.at[chunk, pl.ds(m * 4 + 2 * half, 2), rows(zl), :], home(chunk, half), out_local.at[chunk, half]
        )

    def landed(chunk, half, part):
        if part == 1:
            for t in range(4):
                send_out(chunk, half, t, 1).wait_recv()
        else:
            for t in range(3):
                send_out(chunk, half, t, 0).wait_recv()
            own_out(chunk, half).wait()

    def c_of(part):
        return 1 - zl if part else zl

    def y_copies(half, part):
        ks, c = pl.ds(2 * half, 2), c_of(part)
        down = pltpu.make_async_remote_copy(
            src_ref=outer.at[ks, c, pl.ds(2, 2)], dst_ref=outer.at[ks, c, pl.ds(6, 2)],
            send_sem=y_send.at[half, part, 0], recv_sem=y_recv.at[half, part, 0],
            device_id=y_left, device_id_type=MESH,
        )
        up = pltpu.make_async_remote_copy(
            src_ref=outer.at[ks, c, pl.ds(4, 2)], dst_ref=outer.at[ks, c, pl.ds(0, 2)],
            send_sem=y_send.at[half, part, 1], recv_sem=y_recv.at[half, part, 1],
            device_id=y_right, device_id_type=MESH,
        )
        return down, up

    def spread(half, part):
        landed(0, half, part)
        for copy in y_copies(half, part):
            copy.start()

    for chunk in range(2):
        for t in range(4):
            if t < 3:
                send_in(chunk, t, 0).wait_recv()
            else:
                own_in(chunk).wait()
            send_in(chunk, t, 1).wait_recv()
            group, _ = partner(t, 0)
            four = jnp.concatenate([arrived[chunk, group * 4 + i] for i in range(4)], axis=1)
            packed = jnp.dot(four, pack[...], preferred_element_type=F32)
            left_out[chunk, group] = (packed[:PAIR, :LANES] * keep_left).astype(BF)
            left[chunk, group, PAIR:, :] = packed[:PAIR, LANES:].astype(BF)
            right[chunk, group, :PAIR, :] = packed[PAIR:, :LANES].astype(BF)
            right_out[chunk, group] = (packed[PAIR:, LANES:] * keep_right).astype(BF)
            for copy in edge_copies(chunk, t):
                copy.start()
        if chunk == 1:
            spread(0, 0)
        for t in range(4):
            for copy in edge_copies(chunk, t):
                copy.wait()

        @pl.loop(0, 8)
        def _(turn):
            half, t = turn // 4, turn % 4
            m_to, _ = partner(t, 0)
            kp = m_to * 2 + half
            start = KPTS - 2 * kp
            main = jnp.concatenate([arrived[chunk, q] for q in range(KPTS)], axis=1)
            total = jnp.dot(
                main, t_main[pl.ds(pl.multiple_of(start * LANES, LANES), KPTS * LANES), :],
                preferred_element_type=F32,
            )
            window = pl.ds(pl.multiple_of(start * SMAX, SMAX), KPTS * SMAX)
            lows = jnp.concatenate([left[chunk, g] for g in range(4)], axis=1)
            total = total + jnp.dot(lows, t_left[window, :], preferred_element_type=F32)
            highs = jnp.concatenate([right[chunk, g] for g in range(4)], axis=1)
            total = total + jnp.dot(highs, t_right[window, :], preferred_element_type=F32)
            total = total.astype(BF)
            made[chunk, 2 * kp] = total[:, :LANES]
            made[chunk, 2 * kp + 1] = total[:, LANES:]

            @pl.when(t < 3)
            def _():
                send_out(chunk, half, t, 0).start()

            @pl.when(t == 3)
            def _():
                own_out(chunk, half).start()
                for near_t in range(4):
                    send_out(chunk, half, near_t, 1).start()

            if chunk == 1:

                @pl.when(turn == 0)
                def _():
                    spread(0, 1)

                @pl.when(turn == 5)
                def _():
                    spread(1, 0)

    spread(1, 1)

    def pair_of(source, half, c, first):
        two = [source[2 * half + j, c, pl.ds(first, 4)].reshape(4 * PAIR, LANES) for j in range(2)]
        return jnp.concatenate(two, axis=1)

    def apply_outer(half, part):
        for copy in y_copies(half, part):
            copy.wait()
        c = c_of(part)

        @pl.loop(0, 2)
        def _(side):
            operand = pair_of(outer, half, c, 4 * side)
            for part in range(2):
                a = 4 * side + 2 * part
                block = jnp.dot(k_outer[rows(2 * side + part, 2 * PAIR), :], operand, preferred_element_type=F32)
                for i in range(2):
                    for j in range(2):
                        out[2 * half + j, a + i, c] = block[i * PAIR : (i + 1) * PAIR, j * LANES : (j + 1) * LANES]

    def apply_inner(half, part):
        landed(1, half, part)
        c = c_of(part)

        @pl.loop(0, 2)
        def _(side):
            operand = pair_of(inner, half, c, 0)
            for part in range(2):
                a = 4 * side + 2 * part
                block = jnp.dot(k_inner[rows(2 * side + part, 2 * PAIR), :], operand, preferred_element_type=F32)
                for i in range(2):
                    for j in range(2):
                        out[2 * half + j, a + i, c] += block[i * PAIR : (i + 1) * PAIR, j * LANES : (j + 1) * LANES]

    apply_outer(0, 0)
    apply_outer(0, 1)
    apply_inner(0, 0)
    apply_outer(1, 0)
    apply_inner(0, 1)
    apply_outer(1, 1)
    apply_inner(1, 0)
    landed(1, 1, 1)
    for chunk in range(2):
        for t, u in steps:
            send_in(chunk, t, u).wait_send()
    for chunk in range(2):
        for half in range(2):
            for t, u in steps:
                send_out(chunk, half, t, u).wait_send()


def finish_kernel(most, last, k_inner, out, block, sems):
    c = 1 - lax.axis_index("energy") % 2
    first = pl.ds(0, 2)
    second = pl.ds(2, 2)
    copies = [
        pltpu.make_async_copy(most.at[first], out.at[first], sems.at[0]),
        pltpu.make_async_copy(most.at[second, :, 1 - c], out.at[second, :, 1 - c], sems.at[1]),
    ]
    for copy in copies:
        copy.start()
    operand = jnp.concatenate([last[2 + j, c].reshape(4 * PAIR, LANES) for j in range(2)], axis=1)
    for side in range(2):
        for part in range(2):
            a = 4 * side + 2 * part
            product = jnp.dot(k_inner[a * PAIR : (a + 2) * PAIR, :], operand, preferred_element_type=F32)
            for i in range(2):
                for j in range(2):
                    block[j, a + i] = most[2 + j, a + i, c] + product[i * PAIR : (i + 1) * PAIR, j * LANES : (j + 1) * LANES]
        atoms = pl.ds(4 * side, 4)
        copy = pltpu.make_async_copy(block.at[:, atoms], out.at[second, atoms, c], sems.at[2 + side])
        copy.start()
        copies.append(copy)
    for copy in copies:
        copy.wait()


def shards(green, neighbours, offsets, emit_weight, absorb_weight, coupling):
    k_count, a_count, components, e_count = green.shape
    hbm = pl.BlockSpec(memory_space=pltpu.HBM)
    dma = pltpu.SemaphoreType.DMA
    regular = pltpu.SemaphoreType.REGULAR
    vmem = pltpu.VMEM
    shape = jax.ShapeDtypeStruct((k_count, a_count, 2, PAIR, e_count), F32)
    in_vmem = pl.BlockSpec(memory_space=vmem)
    most, last, k_inner = pl.pallas_call(
        exchange_kernel,
        out_shape=(
            shape,
            jax.ShapeDtypeStruct((k_count, 2, 4, PAIR, LANES), BF),
            jax.ShapeDtypeStruct((a_count * PAIR, 4 * PAIR), BF),
        ),
        in_specs=[hbm] * 6,
        out_specs=(in_vmem,) * 3,
        scratch_shapes=[
            vmem((2, KPTS, 2 * PAIR, LANES), BF),
            vmem((2, KPTS, 2 * PAIR, LANES), BF),
            vmem((2, 4, 2 * PAIR, LANES), BF),
            vmem((2, 4, 2 * PAIR, LANES), BF),
            vmem((2, 4, PAIR, LANES), BF),
            vmem((2, 4, PAIR, LANES), BF),
            vmem((k_count, 2, 8, PAIR, LANES), BF),
            vmem((KPTS, 2 * LANES), F32),
            vmem((2 * KPTS * LANES, 2 * LANES), BF),
            vmem((2 * KPTS * SMAX, 2 * LANES), BF),
            vmem((2 * KPTS * SMAX, 2 * LANES), BF),
            vmem((4 * LANES, 2 * LANES), BF),
            vmem((a_count * PAIR, 4 * PAIR), BF),
            pltpu.SMEM((a_count, NB), jnp.int32),
            pltpu.SMEM((KPTS,), jnp.int32),
            vmem((KPTS, KPTS), BF),
            vmem((KPTS, KPTS), BF),
            vmem((a_count, ORB, NB, ORB), BF),
            vmem((NB, 2, PAIR, ORB * NB), BF),
            vmem((k_count, a_count, 2, PAIR, LANES), BF),
            dma((2, 4, 2)), dma((2, 4, 2)), dma((2,)),
            dma((2, 4, 2)), dma((2, 4, 2)),
            dma((2, 2, 4, 2)), dma((2, 2, 4, 2)), dma((2, 2)),
            dma((2, 2, 2)), dma((2, 2, 2)), dma((6,)),
            regular, regular,
        ],
        compiler_params=pltpu.CompilerParams(
            collective_id=0, has_side_effects=True, vmem_limit_bytes=40 * 1024 * 1024
        ),
        name="exchange",
    )(
        *(
            pltpu.with_memory_space_constraint(array, pltpu.HBM)
            for array in (
                green.reshape(k_count, a_count, 2, PAIR, e_count),
                neighbours,
                offsets,
                emit_weight,
                absorb_weight,
                coupling.transpose(0, 2, 1, 3),
            )
        )
    )
    out = pl.pallas_call(
        finish_kernel,
        out_shape=shape,
        in_specs=[in_vmem] * 3,
        out_specs=hbm,
        scratch_shapes=[vmem((2, a_count, PAIR, LANES), F32), dma((4,))],
        compiler_params=pltpu.CompilerParams(vmem_limit_bytes=8 * 1024 * 1024),
        name="finish",
    )(most, last, k_inner)
    return out.reshape(k_count, a_count, components, e_count)


def solution(mesh):
    in_specs = (
        P("momentum", "atom", None, "energy"),
        P("atom", None),
        P(),
        P(),
        P(),
        P("atom", None, None, None),
    )
    out_specs = P("momentum", "atom", None, "energy")
    return jax.shard_map(shards, mesh=mesh, in_specs=in_specs, out_specs=out_specs, check_vma=False)
```
